256 devices in a mesh: sector: 32 (over x, z_lo, core), layer: 8 (over y, z_hi).
Axes of the slice: x: 4, y: 4, z: 8 (z_hi: 2, z_lo: 4; z = z_hi * 4 + z_lo), core: 2. Of those that a mesh axis runs over, the one named last changes fastest.
Arguments:
- rotor_state: float32 [5, 8, 128, 16384], P(None, None, 'layer', 'sector'), may hold values from -1.5 to 4, as said below
- cavity_state: float32 [5, 4, 128, 16384], P(None, None, 'layer', 'sector'), may hold values from -1.5 to 4, as said below
- block_map: int32 [32], replicated, may hold values from 0 to 31, each once
- rotor_offset: int32 [1], replicated, may hold values from 0 to 511
Outputs:
- rotor_next: float32 [5, 8, 128, 16384], P(None, None, 'layer', 'sector')
- cavity_next: float32 [5, 4, 128, 16384], P(None, None, 'layer', 'sector')
The draws below stay inside these ranges and needn't reach their ends.
Inputs may be any that keep to these rules, and one draw needn't show every extreme that they name: `rotor_state`: component 0 lies in 0.5 to 1.5, components 1 to 3 in -1.5 to 1.5, component 4 in 2 to 4. `cavity_state`: component 0 lies in 0.5 to 1.5, components 1 to 3 in -1.5 to 1.5, component 4 in 2 to 4. `block_map`: each of 0 to 31 once.
All inputs are finite; a program needn't handle non-finite values.
Results may differ from the reference program's by a relative error of at most 0.00002.
Values sent between devices are 32-bit elements; how exact they have to be, the bound alone decides.
A program may use at most 192 MiB of HBM per device.

```python
import jax
import jax.numpy as jnp
from jax import lax

AR = 8
AS = 4
BW = 16
NR = 128
CTH = 512
NTH = 16384
N_SECTOR = 32


def draw_region(key, planes):
    keys = jax.random.split(key, 3)
    density = jax.random.uniform(keys[0], (1, planes, NR, NTH), jnp.float32, 0.6, 1.4)
    momentum = jnp.clip(0.5 * jax.random.normal(keys[1], (3, planes, NR, NTH), jnp.float32), -1.5, 1.5)
    energy = jax.random.uniform(keys[2], (1, planes, NR, NTH), jnp.float32, 2.2, 3.8)
    return jnp.concatenate([density, momentum, energy], axis=0)


def draw_rotor_state(key, part):
    return draw_region(jax.random.fold_in(key, 11), AR)


def draw_cavity_state(key, part):
    return draw_region(jax.random.fold_in(key, 23), AS)


def setup_inputs(seed: int = 0) -> dict:
    splits = jax.random.split(jax.random.key(seed), 5)
    rotor_state = draw_rotor_state(jax.random.fold_in(splits[4], 71), 0)
    cavity_state = draw_cavity_state(jax.random.fold_in(splits[4], 71), 0)
    block_map = jax.random.permutation(splits[2], N_SECTOR).astype(jnp.int32)
    rotor_offset = jax.random.randint(splits[3], (1,), 0, CTH).astype(jnp.int32)
    return {"rotor_state": rotor_state, "cavity_state": cavity_state, "block_map": block_map, "rotor_offset": rotor_offset}


DIFFUSION = 0.05
COURANT = 0.1


def viscosity(density, energy):
    return 0.5 * (energy / density) ** 0.7


def region_update(region, seam_ghost, seam_last):
    viscous = viscosity(region[0], region[4])
    velocity = region[3] / region[0]
    ghost_viscous = viscosity(seam_ghost[0], seam_ghost[4])
    if seam_last:
        extended_mu = jnp.concatenate([viscous, ghost_viscous[None]], axis=0)
    else:
        extended_mu = jnp.concatenate([ghost_viscous[None], viscous], axis=0)

    def component_update(members):
        values, seam_rim = members
        if seam_last:
            extended = jnp.concatenate([values, seam_rim[None]], axis=0)
        else:
            extended = jnp.concatenate([seam_rim[None], values], axis=0)
        face_axial = 0.5 * (extended_mu[1:] + extended_mu[:-1]) * (extended[1:] - extended[:-1])
        empty_plane = jnp.zeros_like(face_axial[:1])
        if seam_last:
            axial_sum = face_axial - jnp.concatenate([empty_plane, face_axial[:-1]], axis=0)
        else:
            axial_sum = jnp.concatenate([face_axial[1:], empty_plane], axis=0) - face_axial
        face_radial = 0.5 * (viscous[:, 1:] + viscous[:, :-1]) * (values[:, 1:] - values[:, :-1])
        empty_face = jnp.zeros_like(face_radial[:, :1])
        radial = jnp.concatenate([face_radial, empty_face], axis=1) - jnp.concatenate([empty_face, face_radial], axis=1)
        face_cycle = 0.5 * (viscous + jnp.roll(viscous, -1, axis=2)) * (jnp.roll(values, -1, axis=2) - values)
        cycle_sum = face_cycle - jnp.roll(face_cycle, 1, axis=2)
        carried = velocity * values
        advected = -COURANT * 0.5 * (jnp.roll(carried, -1, axis=2) - jnp.roll(carried, 1, axis=2))
        return values + DIFFUSION * (axial_sum + radial + cycle_sum) + advected

    return lax.map(component_update, (region, seam_ghost))


def reference(rotor_state, cavity_state, block_map, rotor_offset):
    blocks = jnp.arange(N_SECTOR, dtype=jnp.int32)
    owners = blocks[:, None]
    components = rotor_state.shape[0]
    rotor_seam = rotor_state[:, -1].reshape(components, NR, N_SECTOR, N_SECTOR, BW)
    source = (owners - block_map[None, :]) % N_SECTOR
    landed = rotor_seam[:, :, source, blocks[None, :], :].reshape(components, NR, NTH)
    cavity_ghost = jnp.roll(landed, rotor_offset[0], axis=2)
    lifted = jnp.roll(cavity_state[:, 0], -rotor_offset[0], axis=2).reshape(components, NR, N_SECTOR, N_SECTOR, BW)
    target = (owners + block_map[None, :]) % N_SECTOR
    rotor_ghost = lifted[:, :, target, blocks[None, :], :].reshape(components, NR, NTH)
    rotor_next = region_update(rotor_state, rotor_ghost, True)
    cavity_next = region_update(cavity_state, cavity_ghost, False)
    return rotor_next, cavity_next
```

```python
import functools

import jax
import jax.numpy as jnp
from jax import lax
from jax.experimental import pallas as pl
from jax.experimental.pallas import tpu as pltpu
from jax.sharding import PartitionSpec as P

DIFFUSION = 0.05
LANES = 128
SUB = 8
MESH = pl.DeviceIdType.MESH


def viscosity(density, energy):
    return 0.5 * jnp.exp(0.7 * jnp.log(energy / density))


def iota(axis):
    return lax.broadcasted_iota(jnp.int32, (SUB, LANES), axis)


def granule_transpose(x):
    sub, granule = iota(0), iota(1) // 16
    for bit in range(3):
        s, g = 1 << bit, 16 << bit
        a = (sub // s) % 2
        b = (granule // s) % 2
        up = pltpu.roll(pltpu.roll(x, g, axis=1), SUB - s, axis=0)
        down = pltpu.roll(pltpu.roll(x, LANES - g, axis=1), s, axis=0)
        x = jnp.where(a == b, x, jnp.where(b == 1, up, down))
    return x


def kernel(
    map_ref, offset_ref, rotor_hbm, cavity_hbm, rotor_out, cavity_out,
    rotor, cavity, rotor_new, cavity_new, mu_r, mu_c, w_r, w_c,
    two_cavity, two_landed, rotor_ghost, cavity_ghost,
    packed, send_r, recv_r, send_c, recv_c,
    low_own, high_own, low_got, high_got, col_own, col_got, inverse,
    load_sem, store_sem, send_r_sem, recv_r_sem, send_c_sem, recv_c_sem, shift_send, shift_recv, edge_send, edge_recv,
):
    sectors = lax.axis_size("sector")
    layers = lax.axis_size("layer")
    me = lax.axis_index("sector")
    layer = lax.axis_index("layer")
    comps, tiles, rows_r, _ = rotor.shape
    rows_c = cavity.shape[2]
    rows = two_cavity.shape[2]
    width = tiles * LANES
    planes_r, planes_c = rows_r // rows, rows_c // rows
    last_r = rows_r - rows
    used = comps * 2

    def sector_at(step):
        return {"sector": lax.rem(me + step + sectors, sectors)}

    loads = []
    for t in range(tiles):
        loads.append(pltpu.make_async_copy(
            rotor_hbm.at[:, pl.ds(last_r, rows), pl.ds(t * LANES, LANES)], two_landed.at[t], load_sem.at[t]))
    for t in range(tiles):
        loads.append(pltpu.make_async_copy(
            cavity_hbm.at[:, pl.ds(0, rows), pl.ds(t * LANES, LANES)], two_cavity.at[t], load_sem.at[tiles + t]))
    for hbm, region, base in ((rotor_hbm, rotor, 2 * tiles), (cavity_hbm, cavity, 3 * tiles)):
        for t in range(tiles):
            loads.append(pltpu.make_async_copy(
                hbm.at[:, :, pl.ds(t * LANES, LANES)], region.at[:, t], load_sem.at[base + t]))
    for copy in loads:
        copy.start()

    barrier = pltpu.get_barrier_semaphore()

    def greet(k, carry):
        pl.semaphore_signal(barrier, inc=1, device_id=sector_at(k), device_id_type=MESH)
        return carry

    lax.fori_loop(1, sectors, greet, 0)

    @pl.when(layer > 0)
    def _():
        pl.semaphore_signal(barrier, inc=1, device_id={"layer": layer - 1}, device_id_type=MESH)

    @pl.when(layer < layers - 1)
    def _():
        pl.semaphore_signal(barrier, inc=1, device_id={"layer": layer + 1}, device_id_type=MESH)

    def invert(k, carry):
        found = jnp.int32(0)
        for j in range(sectors):
            found = jnp.where(map_ref[j] == k, jnp.int32(j), found)
        inverse[k] = found
        return carry

    lax.fori_loop(0, sectors, invert, 0)

    def pack(source, base, send, recv):
        def one(t, carry):
            for q in range(used):
                tile = source[base + t, q // 2, pl.ds(SUB * (q % 2), SUB), :]
                packed[pl.ds(SUB * t, SUB), q, :] = granule_transpose(tile)
            return carry

        lax.fori_loop(0, tiles, one, 0)
        recv[0] = packed[inverse[0]]

        def slot(k, carry):
            send[k] = packed[inverse[k]]
            return carry

        lax.fori_loop(1, sectors, slot, 0)

    def unpack(recv, target, base):
        def block(j, carry):
            packed[j] = recv[map_ref[j]]
            return carry

        lax.fori_loop(0, sectors, block, 0)

        def one(t, carry):
            for q in range(used):
                tile = packed[pl.ds(SUB * t, SUB), q, :]
                target[base + t, q // 2, pl.ds(SUB * (q % 2), SUB), :] = granule_transpose(tile)
            return carry

        lax.fori_loop(0, tiles, one, 0)

    def block_copy(send, recv, send_sem, recv_sem, k, sign):
        return pltpu.make_async_remote_copy(
            src_ref=send.at[k, pl.ds(0, used)], dst_ref=recv.at[k, pl.ds(0, used)],
            send_sem=send_sem.at[k], recv_sem=recv_sem.at[k],
            device_id=sector_at(sign * k), device_id_type=MESH)

    def start_blocks(send, recv, send_sem, recv_sem, sign):
        def one(k, carry):
            block_copy(send, recv, send_sem, recv_sem, k, sign).start()
            return carry

        lax.fori_loop(1, sectors, one, 0)

    def wait_blocks(send, recv, send_sem, recv_sem, sign, arrived):
        def one(k, carry):
            copy = block_copy(send, recv, send_sem, recv_sem, k, sign)
            if arrived:
                copy.wait_recv()
            else:
                copy.wait_send()
            return carry

        lax.fori_loop(1, sectors, one, 0)

    def shift_copy(buffer, source, target, index, step):
        return pltpu.make_async_remote_copy(
            src_ref=buffer.at[pl.ds(source, tiles)], dst_ref=buffer.at[pl.ds(target, tiles)],
            send_sem=shift_send.at[index], recv_sem=shift_recv.at[index],
            device_id=sector_at(step), device_id_type=MESH)

    def shifted(buffer, target, start):
        tile0 = lax.div(start, jnp.int32(LANES))
        rest = lax.rem(start, jnp.int32(LANES))
        back = lax.rem(LANES - rest, jnp.int32(LANES))
        keep = lax.broadcasted_iota(jnp.int32, (rows, LANES), 1) < LANES - rest
        for t in range(tiles):
            i0 = tile0 + t
            i1 = jnp.minimum(i0 + 1, 2 * tiles - 1)
            for c in range(comps):
                here = pltpu.roll(buffer[i0, c], back, axis=1)
                after = pltpu.roll(buffer[i1, c], back, axis=1)
                target[t, c] = jnp.where(keep, here, after)

    offset = offset_ref[0]

    for t in range(tiles):
        loads[t].wait()
    pack(two_landed, 0, send_r, recv_r)
    for t in range(tiles):
        loads[tiles + t].wait()

    pl.semaphore_wait(barrier, sectors - 1 + jnp.where(layer > 0, 1, 0) + jnp.where(layer < layers - 1, 1, 0))

    cavity_shift = shift_copy(two_cavity, 0, tiles, 0, -1)
    cavity_shift.start()
    start_blocks(send_r, recv_r, send_r_sem, recv_r_sem, 1)

    for copy in loads[2 * tiles:]:
        copy.wait()

    first_c = comps * tiles * planes_r
    for edge, own in ((0, low_own), (rows - 1, high_own)):
        for c in range(comps):
            for t in range(tiles):
                own[pl.ds((c * tiles + t) * planes_r, planes_r), :] = rotor[c, t, pl.ds(edge, planes_r, stride=rows), :]
                own[pl.ds(first_c + (c * tiles + t) * planes_c, planes_c), :] = cavity[
                    c, t, pl.ds(edge, planes_c, stride=rows), :]

    up_copy = pltpu.make_async_remote_copy(
        src_ref=high_own, dst_ref=low_got, send_sem=edge_send.at[0], recv_sem=edge_recv.at[0],
        device_id={"layer": lax.rem(layer + 1, layers)}, device_id_type=MESH)
    down_copy = pltpu.make_async_remote_copy(
        src_ref=low_own, dst_ref=high_got, send_sem=edge_send.at[1], recv_sem=edge_recv.at[1],
        device_id={"layer": lax.rem(layer + layers - 1, layers)}, device_id_type=MESH)

    @pl.when(layer < layers - 1)
    def _():
        up_copy.start()

    @pl.when(layer > 0)
    def _():
        down_copy.start()

    lane = iota(1)
    pieces = []
    for c in range(comps):
        for region, new, planes in ((rotor, rotor_new, planes_r), (cavity, cavity_new, planes_c)):
            for p in range(planes):
                for half in range(2):
                    pieces.append((region, new, c, p * rows + half * SUB))
    group = len(pieces) // comps
    zero = jnp.zeros((SUB, LANES), jnp.float32)
    head, tail = zero, zero
    for v, (region, _, c, r) in enumerate(pieces):
        head = jnp.where(lane == v, region[c, 0, pl.ds(r, SUB), :][:, 0:1], head)
        tail = jnp.where(lane == v, region[c, tiles - 1, pl.ds(r, SUB), :][:, LANES - 1:], tail)
    col_own[0] = head
    col_own[1] = tail
    col_copies = [
        pltpu.make_async_remote_copy(
            src_ref=col_own.at[i], dst_ref=col_got.at[i], send_sem=edge_send.at[2 + i], recv_sem=edge_recv.at[2 + i],
            device_id=sector_at(-1 if i == 0 else 1), device_id_type=MESH)
        for i in range(2)
    ]
    for copy in col_copies:
        copy.start()

    rate = jnp.float32(DIFFUSION)
    half_rate = jnp.float32(0.5 * DIFFUSION)
    wide_lane = lax.broadcasted_iota(jnp.int32, (rows, width), 1)
    wide_row = lax.broadcasted_iota(jnp.int32, (rows, width), 0)

    def whole(region, c, at):
        return jnp.concatenate([region[c, t, at, :] for t in range(tiles)], axis=1)

    def interior(region, new, mu, w, planes):
        def first(p, carry):
            at = pl.ds(pl.multiple_of(p * rows, rows), rows)
            density = whole(region, 0, at)
            mu[p] = viscosity(density, whole(region, 4, at))
            w[p] = whole(region, 3, at) / density
            return carry

        lax.fori_loop(0, planes, first, 0)

        def one(p, carry):
            at = pl.ds(pl.multiple_of(p * rows, rows), rows)
            above = jnp.minimum(p + 1, planes - 1)
            below = jnp.maximum(p - 1, 0)
            at_above = pl.ds(pl.multiple_of(above * rows, rows), rows)
            at_below = pl.ds(pl.multiple_of(below * rows, rows), rows)
            m = mu[p]
            up = half_rate * (m + mu[above])
            down = half_rate * (m + mu[below])
            radial = jnp.where(wide_row == rows - 1, 0.0, half_rate * (m + pltpu.roll(m, rows - 1, axis=0)))
            cycle = half_rate * (m + pltpu.roll(m, width - 1, axis=1))
            speed = rate * w[p]
            ahead = pltpu.roll(speed, width - 1, axis=1)
            inner = wide_lane < width - 1
            next_factor = jnp.where(inner, cycle - ahead, 0.0)
            here_factor = jnp.where(inner, cycle + speed, 0.0)
            for c in range(comps):
                q = whole(region, c, at)
                total = q + up * (whole(region, c, at_above) - q) + down * (whole(region, c, at_below) - q)
                face = radial * (pltpu.roll(q, rows - 1, axis=0) - q)
                total = total + (face - pltpu.roll(face, 1, axis=0))
                face = next_factor * pltpu.roll(q, width - 1, axis=1) - here_factor * q
                total = total + (face - pltpu.roll(face, 1, axis=1))
                for t in range(tiles):
                    new[c, t, at, :] = total[:, t * LANES:(t + 1) * LANES]
            return carry

        lax.fori_loop(0, planes, one, 0)

    interior(rotor, rotor_new, mu_r, w_r, planes_r)
    interior(cavity, cavity_new, mu_c, w_c, planes_c)

    cavity_shift.wait_recv()
    shifted(two_cavity, rotor_ghost, offset)
    pack(rotor_ghost, 0, send_c, recv_c)
    start_blocks(send_c, recv_c, send_c_sem, recv_c_sem, -1)

    wait_blocks(send_r, recv_r, send_r_sem, recv_r_sem, 1, True)
    unpack(recv_r, two_landed, tiles)
    landed_shift = shift_copy(two_landed, tiles, 0, 1, 1)
    landed_shift.start()

    def edge_fix(own, got, edge):
        for region, new, planes, base in ((rotor, rotor_new, planes_r, 0), (cavity, cavity_new, planes_c, first_c)):
            size = tiles * planes
            a = [own[pl.ds(base + c * size, size), :] for c in range(comps)]
            b = [got[pl.ds(base + c * size, size), :] for c in range(comps)]
            factor = half_rate * (viscosity(a[0], a[4]) + viscosity(b[0], b[4]))
            for c in range(comps):
                change = factor * (b[c] - a[c])
                for t in range(tiles):
                    at = (c, t, pl.ds(edge, planes, stride=rows), slice(None))
                    new[at] = new[at] + change[t * planes:(t + 1) * planes]

    @pl.when(layer < layers - 1)
    def _():
        down_like = pltpu.make_async_remote_copy(
            src_ref=low_own, dst_ref=high_got, send_sem=edge_send.at[1], recv_sem=edge_recv.at[1],
            device_id={"layer": lax.rem(layer + 1, layers)}, device_id_type=MESH)
        down_like.wait_recv()
        edge_fix(high_own, high_got, rows - 1)

    @pl.when(layer > 0)
    def _():
        up_like = pltpu.make_async_remote_copy(
            src_ref=high_own, dst_ref=low_got, send_sem=edge_send.at[0], recv_sem=edge_recv.at[0],
            device_id={"layer": lax.rem(layer + layers - 1, layers)}, device_id_type=MESH)
        up_like.wait_recv()
        edge_fix(low_own, low_got, 0)

    for copy in col_copies:
        copy.wait_recv()

    def spread(x, shift):
        one = jnp.where(lane < group, pltpu.roll(x, LANES - shift, axis=1) if shift else x, 0.0)
        out = one
        for c in range(1, comps):
            out = out + pltpu.roll(one, c * group, axis=1)
        return out

    def column_state(x):
        density, momentum, energy = spread(x, 0), spread(x, 3 * group), spread(x, 4 * group)
        live = lane < comps * group
        density = jnp.where(live, density, 1.0)
        energy = jnp.where(live, energy, 1.0)
        return viscosity(density, energy), momentum / density

    states = {}
    for name, x in (("head", col_own[0]), ("tail", col_own[1]), ("after", col_got[0]), ("before", col_got[1])):
        states[name] = (x, *column_state(x))

    def column_face(a, b):
        (qa, ma, wa), (qb, mb, wb) = states[a], states[b]
        return half_rate * (ma + mb) * (qb - qa) - rate * (wa * qa + wb * qb)

    at_tail = column_face("tail", "after")
    at_head = column_face("before", "head")
    for v, (_, new, c, r) in enumerate(pieces):
        at = (c, tiles - 1, pl.ds(r, SUB), slice(None))
        new[at] = new[at] + jnp.where(lane == LANES - 1, at_tail[:, v:v + 1], 0.0)
        at = (c, 0, pl.ds(r, SUB), slice(None))
        new[at] = new[at] - jnp.where(lane == 0, at_head[:, v:v + 1], 0.0)

    stores = []
    for new, out, low, size in (
        (rotor_new, rotor_out, 0, last_r), (cavity_new, cavity_out, rows, rows_c - rows),
        (rotor_new, rotor_out, last_r, rows), (cavity_new, cavity_out, 0, rows),
    ):
        at = pl.ds(low, size)
        stores.append([
            pltpu.make_async_copy(
                new.at[:, t, at], out.at[:, at, pl.ds(t * LANES, LANES)], store_sem.at[len(stores) * tiles + t])
            for t in range(tiles)
        ])

    def store(index):
        for copy in stores[index]:
            copy.start()

    store(0)
    store(1)

    def seam_fix(region, new, mu, p, ghost):
        for t in range(tiles):
            lanes = pl.ds(t * LANES, LANES)
            factor = half_rate * (viscosity(ghost[t, 0], ghost[t, 4]) + mu[p, :, lanes])
            for c in range(comps):
                at = (c, t, pl.ds(p * rows, rows), slice(None))
                new[at] = new[at] + factor * (ghost[t, c] - region[at])

    wait_blocks(send_c, recv_c, send_c_sem, recv_c_sem, -1, True)
    unpack(recv_c, rotor_ghost, 0)
    seam_fix(rotor, rotor_new, mu_r, planes_r - 1, rotor_ghost)
    store(2)

    landed_shift.wait_recv()
    shifted(two_landed, cavity_ghost, width - offset)
    seam_fix(cavity, cavity_new, mu_c, 0, cavity_ghost)
    store(3)

    cavity_shift.wait_send()
    landed_shift.wait_send()
    wait_blocks(send_r, recv_r, send_r_sem, recv_r_sem, 1, False)
    wait_blocks(send_c, recv_c, send_c_sem, recv_c_sem, -1, False)
    for copy in col_copies:
        copy.wait_send()

    @pl.when(layer < layers - 1)
    def _():
        up_copy.wait_send()

    @pl.when(layer > 0)
    def _():
        down_copy.wait_send()

    for copies in stores:
        for copy in copies:
            copy.wait()


def shards(sectors, rotor_state, cavity_state, block_map, rotor_offset):
    comps, planes_r, rows, width = rotor_state.shape
    planes_c = cavity_state.shape[1]
    tiles = width // LANES
    rotor = rotor_state.reshape(comps, planes_r * rows, width)
    cavity = cavity_state.reshape(comps, planes_c * rows, width)
    f32 = jnp.float32
    edge_rows = comps * tiles * (planes_r + planes_c)
    dma = pltpu.SemaphoreType.DMA
    anywhere = pl.BlockSpec(memory_space=pl.ANY)
    scalar = pl.BlockSpec(memory_space=pltpu.SMEM)
    block = pltpu.VMEM((sectors, 16, LANES), f32)
    tiled_r = pltpu.VMEM((comps, tiles, planes_r * rows, LANES), f32)
    tiled_c = pltpu.VMEM((comps, tiles, planes_c * rows, LANES), f32)
    edge = pltpu.VMEM((edge_rows, LANES), f32)
    columns = pltpu.VMEM((2, SUB, LANES), f32)
    rotor_next, cavity_next = pl.pallas_call(
        kernel,
        out_shape=(jax.ShapeDtypeStruct(rotor.shape, f32), jax.ShapeDtypeStruct(cavity.shape, f32)),
        in_specs=[scalar, scalar, anywhere, anywhere],
        out_specs=(anywhere, anywhere),
        scratch_shapes=[
            tiled_r, tiled_c, tiled_r, tiled_c,
            pltpu.VMEM((planes_r, rows, width), f32), pltpu.VMEM((planes_c, rows, width), f32),
            pltpu.VMEM((planes_r, rows, width), f32), pltpu.VMEM((planes_c, rows, width), f32),
            pltpu.VMEM((2 * tiles, comps, rows, LANES), f32), pltpu.VMEM((2 * tiles, comps, rows, LANES), f32),
            pltpu.VMEM((tiles, comps, rows, LANES), f32), pltpu.VMEM((tiles, comps, rows, LANES), f32),
            block, block, block, block, block,
            edge, edge, edge, edge, columns, columns,
            pltpu.SMEM((sectors,), jnp.int32),
            dma((4 * tiles,)), dma((4 * tiles,)), dma((sectors,)), dma((sectors,)), dma((sectors,)), dma((sectors,)),
            dma((2,)), dma((2,)), dma((4,)), dma((4,)),
        ],
        compiler_params=pltpu.CompilerParams(collective_id=0, has_side_effects=True),
    )(block_map, rotor_offset, rotor, cavity)
    return rotor_next.reshape(rotor_state.shape), cavity_next.reshape(cavity_state.shape)


def solution(mesh):
    placed = (P(None, None, "layer", "sector"), P(None, None, "layer", "sector"), P(), P())
    return jax.shard_map(
        functools.partial(shards, mesh.shape["sector"]),
        mesh=mesh,
        in_specs=placed,
        out_specs=(P(None, None, "layer", "sector"), P(None, None, "layer", "sector")),
        check_vma=False,
    )
```

```python
import functools

import jax
import jax.numpy as jnp
from jax import lax
from jax.experimental import pallas as pl
from jax.experimental.pallas import tpu as pltpu
from jax.sharding import PartitionSpec as P

DIFFUSION = 0.05
LANES = 128
SUB = 8
PAD = 8
PIECES = 10
EARLY = 2
MESH = pl.DeviceIdType.MESH


def viscosity(density, energy):
    return 0.5 * jnp.exp(0.7 * jnp.log(energy / density))


def iota(axis):
    return lax.broadcasted_iota(jnp.int32, (SUB, LANES), axis)


def granule_transpose(x):
    sub, granule = iota(0), iota(1) // 16
    for bit in range(3):
        s, g = 1 << bit, 16 << bit
        a = (sub // s) % 2
        b = (granule // s) % 2
        up = pltpu.roll(pltpu.roll(x, g, axis=1), SUB - s, axis=0)
        down = pltpu.roll(pltpu.roll(x, LANES - g, axis=1), s, axis=0)
        x = jnp.where(a == b, x, jnp.where(b == 1, up, down))
    return x


def kernel(
    map_hbm, offset_ref, rotor_hbm, cavity_hbm, rotor_new, cavity_new,
    rotor, cavity, mu_r, mu_c, w_r, w_c,
    two_cavity, two_landed, rotor_ghost, cavity_ghost,
    packed, send_r, recv_r, send_c, recv_c,
    low_own, high_own, low_got, high_got, col_own, col_got, inverse_v, inverse,
    map_ref, load_sem, send_r_sem, recv_r_sem, send_c_sem, recv_c_sem, shift_send, shift_recv, edge_send, edge_recv,
    col_send, col_recv,
):
    sectors = lax.axis_size("sector")
    layers = lax.axis_size("layer")
    me = lax.axis_index("sector")
    layer = lax.axis_index("layer")
    comps, tiles, rows_r, _ = rotor_new.shape
    rows_c = cavity_new.shape[2]
    rows = two_cavity.shape[2]
    width = tiles * LANES
    planes_r, planes_c = rows_r // rows, rows_c // rows
    last_r = rows_r - rows
    used = comps * 2
    slot_rows = send_r.shape[1]
    packed_rows = packed.reshape(sectors * slot_rows, LANES)

    def sector_at(step):
        return {"sector": lax.rem(me + step + sectors, sectors)}

    loads = []
    for t in range(tiles):
        loads.append(pltpu.make_async_copy(
            rotor_hbm.at[:, pl.ds(last_r, rows), pl.ds(t * LANES, LANES)], two_landed.at[t], load_sem.at[t]))
    for t in range(tiles):
        loads.append(pltpu.make_async_copy(
            cavity_hbm.at[:, pl.ds(0, rows), pl.ds(t * LANES, LANES)], two_cavity.at[t], load_sem.at[tiles + t]))
    for hbm, region, base in ((rotor_hbm, rotor, 2 * tiles), (cavity_hbm, cavity, 3 * tiles)):
        for t in range(tiles):
            loads.append(pltpu.make_async_copy(
                hbm.at[:, :, pl.ds(t * LANES, LANES)], region.at[:, t, pl.ds(PAD, hbm.shape[1])], load_sem.at[base + t]))
    map_load = pltpu.make_async_copy(map_hbm, map_ref, load_sem.at[4 * tiles + 1])
    map_load.start()
    for copy in loads:
        copy.start()

    barrier = pltpu.get_barrier_semaphore()

    def greet(k, carry):
        pl.semaphore_signal(barrier, inc=1, device_id=sector_at(k), device_id_type=MESH)
        return carry

    lax.fori_loop(1, sectors, greet, 0)

    @pl.when(layer > 0)
    def _():
        pl.semaphore_signal(barrier, inc=1, device_id={"layer": layer - 1}, device_id_type=MESH)

    @pl.when(layer < layers - 1)
    def _():
        pl.semaphore_signal(barrier, inc=1, device_id={"layer": layer + 1}, device_id_type=MESH)

    map_load.wait()

    found = jnp.zeros((SUB, LANES), jnp.int32)
    for j in range(sectors):
        found = jnp.where(iota(1) == map_ref[j], j, found)
    inverse_v[...] = found

    for region in (rotor, cavity):
        for c in range(comps):
            for t in range(tiles):
                region[c, t, pl.ds(0, PAD), :] = jnp.zeros((PAD, LANES), jnp.float32)
                region[c, t, pl.ds(region.shape[2] - PAD, PAD), :] = jnp.zeros((PAD, LANES), jnp.float32)

    to_scalar = pltpu.make_async_copy(inverse_v, inverse, load_sem.at[4 * tiles])
    to_scalar.start()

    def pack(read, send, recv):
        def one(t, carry):
            for q in range(used):
                packed_rows[pl.ds(SUB * slot_rows * t + q, SUB, stride=slot_rows), :] = granule_transpose(read(t, q))
            return carry

        lax.fori_loop(0, tiles, one, 0)

        recv[0] = packed[inverse[0, 0]]

        def slot(k, carry):
            send[k] = packed[inverse[0, k]]
            return carry

        lax.fori_loop(1, sectors, slot, 0)

    def unpack(recv, write):
        def block(j, carry):
            packed[j] = recv[map_ref[j]]
            return carry

        lax.fori_loop(0, sectors, block, 0)

        def one(t, carry):
            for q in range(used):
                write(t, q, granule_transpose(packed_rows[pl.ds(SUB * slot_rows * t + q, SUB, stride=slot_rows), :]))
            return carry

        lax.fori_loop(0, tiles, one, 0)

    def seam_reader(buffer):
        return lambda t, q: buffer[t, q // 2, pl.ds(SUB * (q % 2), SUB), :]

    def seam_writer(buffer, base):
        def write(t, q, value):
            buffer[base + t, q // 2, pl.ds(SUB * (q % 2), SUB), :] = value

        return write

    def block_copy(send, recv, send_sem, recv_sem, k, sign):
        return pltpu.make_async_remote_copy(
            src_ref=send.at[k, pl.ds(0, used)], dst_ref=recv.at[k, pl.ds(0, used)],
            send_sem=send_sem.at[k], recv_sem=recv_sem.at[k],
            device_id=sector_at(sign * k), device_id_type=MESH)

    def start_blocks(send, recv, send_sem, recv_sem, sign):
        def one(k, carry):
            block_copy(send, recv, send_sem, recv_sem, k, sign).start()
            return carry

        lax.fori_loop(1, sectors, one, 0)

    def wait_blocks(send, recv, send_sem, recv_sem, sign, arrived):
        def one(k, carry):
            copy = block_copy(send, recv, send_sem, recv_sem, k, sign)
            if arrived:
                copy.wait_recv()
            else:
                copy.wait_send()
            return carry

        lax.fori_loop(1, sectors, one, 0)

    def shift_copy(buffer, source, target, index, step):
        return pltpu.make_async_remote_copy(
            src_ref=buffer.at[pl.ds(source, tiles)], dst_ref=buffer.at[pl.ds(target, tiles)],
            send_sem=shift_send.at[index], recv_sem=shift_recv.at[index],
            device_id=sector_at(step), device_id_type=MESH)

    def shifted(buffer, target, start):
        tile0 = lax.div(start, jnp.int32(LANES))
        rest = lax.rem(start, jnp.int32(LANES))
        back = lax.rem(LANES - rest, jnp.int32(LANES))
        keep = lax.broadcasted_iota(jnp.int32, (rows, LANES), 1) < LANES - rest
        for t in range(tiles):
            i0 = tile0 + t
            i1 = jnp.minimum(i0 + 1, 2 * tiles - 1)
            for c in range(comps):
                here = pltpu.roll(buffer[i0, c], back, axis=1)
                after = pltpu.roll(buffer[i1, c], back, axis=1)
                target[t, c] = jnp.where(keep, here, after)

    offset = offset_ref[0]

    for t in range(tiles):
        loads[t].wait()
    to_scalar.wait()
    pack(seam_reader(two_landed), send_r, recv_r)
    for t in range(tiles):
        loads[tiles + t].wait()

    for copy in loads[2 * tiles:]:
        copy.wait()

    first_c = comps * tiles * planes_r
    for edge, own in ((0, low_own), (rows - 1, high_own)):
        for c in range(comps):
            for t in range(tiles):
                own[pl.ds((c * tiles + t) * planes_r, planes_r), :] = rotor[c, t, pl.ds(PAD + edge, planes_r, stride=rows), :]
                own[pl.ds(first_c + (c * tiles + t) * planes_c, planes_c), :] = cavity[
                    c, t, pl.ds(PAD + edge, planes_c, stride=rows), :]

    lane = iota(1)
    pieces = []
    for c in range(comps):
        for region, new, planes in ((rotor, rotor_new, planes_r), (cavity, cavity_new, planes_c)):
            for p in range(planes):
                for half in range(2):
                    pieces.append((region, new, c, p * rows + half * SUB))
    group = len(pieces) // comps
    zero = jnp.zeros((SUB, LANES), jnp.float32)
    head, tail = zero, zero
    for v, (region, _, c, r) in enumerate(pieces):
        head = jnp.where(lane == v, region[c, 0, pl.ds(PAD + r, SUB), :][:, 0:1], head)
        tail = jnp.where(lane == v, region[c, tiles - 1, pl.ds(PAD + r, SUB), :][:, LANES - 1:], tail)
    col_own[0] = head
    col_own[1] = tail
    pl.semaphore_wait(barrier, sectors - 1 + jnp.where(layer > 0, 1, 0) + jnp.where(layer < layers - 1, 1, 0))

    cavity_shift = shift_copy(two_cavity, 0, tiles, 0, -1)
    cavity_shift.start()
    start_blocks(send_r, recv_r, send_r_sem, recv_r_sem, 1)

    col_copies = [
        pltpu.make_async_remote_copy(
            src_ref=col_own.at[i], dst_ref=col_got.at[i], send_sem=col_send.at[i], recv_sem=col_recv.at[i],
            device_id=sector_at(-1 if i == 0 else 1), device_id_type=MESH)
        for i in range(2)
    ]
    for copy in col_copies:
        copy.start()

    edge_rows = low_own.shape[0] // PIECES

    def edge_copy(upward, piece, step):
        source, target = (high_own, low_got) if upward else (low_own, high_got)
        at = pl.ds(piece * edge_rows, edge_rows)
        return pltpu.make_async_remote_copy(
            src_ref=source.at[at], dst_ref=target.at[at],
            send_sem=edge_send.at[upward, piece], recv_sem=edge_recv.at[upward, piece],
            device_id={"layer": lax.rem(layer + step + layers, layers)}, device_id_type=MESH)

    def start_edges(low, high):
        @pl.when(layer < layers - 1)
        def _():
            for piece in range(low, high):
                edge_copy(1, piece, 1).start()

        @pl.when(layer > 0)
        def _():
            for piece in range(low, high):
                edge_copy(0, piece, -1).start()

    start_edges(0, EARLY)

    rate = jnp.float32(DIFFUSION)
    half_rate = jnp.float32(0.5 * DIFFUSION)
    row = lax.broadcasted_iota(jnp.int32, (rows, LANES), 0)
    column = lax.broadcasted_iota(jnp.int32, (rows, LANES), 1)

    def interior(region, new, mu, w, planes):
        def first(p, carry):
            at = pl.ds(pl.multiple_of(PAD + p * rows, SUB), rows)
            for t in range(tiles):
                density = region[0, t, at, :]
                mu[t, at, :] = viscosity(density, region[4, t, at, :])
                w[t, at, :] = region[3, t, at, :] / density
            return carry

        lax.fori_loop(0, planes, first, 0)

        def one(p, carry):
            base = pl.multiple_of(PAD + p * rows, SUB)
            at = pl.ds(base, rows)
            upper, lower = pl.ds(base + 1, rows), pl.ds(base - 1, rows)
            above = pl.ds(pl.multiple_of(PAD + jnp.minimum(p + 1, planes - 1) * rows, SUB), rows)
            below = pl.ds(pl.multiple_of(PAD + jnp.maximum(p - 1, 0) * rows, SUB), rows)
            rate_above = jnp.where(p < planes - 1, half_rate, 0.0)
            rate_below = jnp.where(p > 0, half_rate, 0.0)

            def after(ref, t):
                x = ref[t, at, :]
                if t < tiles - 1:
                    x = jnp.where(column == 0, ref[t + 1, at, :], x)
                return pltpu.roll(x, LANES - 1, axis=1)

            def before(ref, t):
                x = ref[t, at, :]
                if t > 0:
                    x = jnp.where(column == LANES - 1, ref[t - 1, at, :], x)
                return pltpu.roll(x, 1, axis=1)

            for t in range(tiles):
                m = mu[t, at, :]
                up = rate_above * (m + mu[t, above, :])
                down = rate_below * (m + mu[t, below, :])
                out = jnp.where(row == rows - 1, 0.0, half_rate * (m + mu[t, upper, :]))
                inn = jnp.where(row == 0, 0.0, half_rate * (m + mu[t, lower, :]))
                east = half_rate * (m + after(mu, t))
                west = half_rate * (m + before(mu, t))
                wind_east = rate * after(w, t)
                wind_west = rate * before(w, t)
                if t == tiles - 1:
                    east = jnp.where(column == LANES - 1, 0.0, east)
                    wind_east = jnp.where(column == LANES - 1, 0.0, wind_east)
                if t == 0:
                    west = jnp.where(column == 0, 0.0, west)
                    wind_west = jnp.where(column == 0, 0.0, wind_west)
                centre = 1.0 - ((up + down) + (out + inn) + (east + west))
                east = east - wind_east
                west = west + wind_west
                for c in range(comps):
                    values = region.at[c]
                    total = centre * values[t, at, :]
                    total = total + (up * values[t, above, :] + down * values[t, below, :])
                    total = total + (out * values[t, upper, :] + inn * values[t, lower, :])
                    total = total + (east * after(values, t) + west * before(values, t))
                    new[c, t, pl.ds(pl.multiple_of(p * rows, rows), rows), :] = total
            return carry

        lax.fori_loop(0, planes, one, 0)

    interior(rotor, rotor_new, mu_r, w_r, planes_r)
    interior(cavity, cavity_new, mu_c, w_c, planes_c)

    cavity_shift.wait_recv()
    shifted(two_cavity, rotor_ghost, offset)
    pack(seam_reader(rotor_ghost), send_c, recv_c)
    start_blocks(send_c, recv_c, send_c_sem, recv_c_sem, -1)

    wait_blocks(send_r, recv_r, send_r_sem, recv_r_sem, 1, True)
    unpack(recv_r, seam_writer(two_landed, tiles))
    landed_shift = shift_copy(two_landed, tiles, 0, 1, 1)
    landed_shift.start()
    start_edges(EARLY, PIECES)

    def edge_fix(own, got, edge):
        for region, new, planes, base in ((rotor, rotor_new, planes_r, 0), (cavity, cavity_new, planes_c, first_c)):
            size = tiles * planes
            a = [own[pl.ds(base + c * size, size), :] for c in range(comps)]
            b = [got[pl.ds(base + c * size, size), :] for c in range(comps)]
            factor = half_rate * (viscosity(a[0], a[4]) + viscosity(b[0], b[4]))
            for c in range(comps):
                change = factor * (b[c] - a[c])
                for t in range(tiles):
                    at = (c, t, pl.ds(edge, planes, stride=rows), slice(None))
                    new[at] = new[at] + change[t * planes:(t + 1) * planes]

    for copy in col_copies:
        copy.wait_recv()

    def spread(x, shift):
        one = jnp.where(lane < group, pltpu.roll(x, LANES - shift, axis=1) if shift else x, 0.0)
        out = one
        for c in range(1, comps):
            out = out + pltpu.roll(one, c * group, axis=1)
        return out

    def column_state(x):
        density, momentum, energy = spread(x, 0), spread(x, 3 * group), spread(x, 4 * group)
        live = lane < comps * group
        density = jnp.where(live, density, 1.0)
        energy = jnp.where(live, energy, 1.0)
        return viscosity(density, energy), momentum / density

    states = {}
    for name, x in (("head", col_own[0]), ("tail", col_own[1]), ("after", col_got[0]), ("before", col_got[1])):
        states[name] = (x, *column_state(x))

    def column_face(a, b):
        (qa, ma, wa), (qb, mb, wb) = states[a], states[b]
        return half_rate * (ma + mb) * (qb - qa), rate * wb * qb

    def column_change(own, other, sign):
        diffused, carried = column_face(own, other)
        return diffused - sign * carried

    at_tail = column_change("tail", "after", 1.0)
    at_head = column_change("head", "before", -1.0)
    for v, (_, new, c, r) in enumerate(pieces):
        at = (c, tiles - 1, pl.ds(r, SUB), slice(None))
        new[at] = new[at] + jnp.where(lane == LANES - 1, at_tail[:, v:v + 1], 0.0)
        at = (c, 0, pl.ds(r, SUB), slice(None))
        new[at] = new[at] + jnp.where(lane == 0, at_head[:, v:v + 1], 0.0)

    def seam_fix(region, new, mu, p, ghost):
        for t in range(tiles):
            inside = pl.ds(PAD + p * rows, rows)
            factor = half_rate * (viscosity(ghost[t, 0], ghost[t, 4]) + mu[t, inside, :])
            for c in range(comps):
                at = (c, t, pl.ds(p * rows, rows), slice(None))
                new[at] = new[at] + factor * (ghost[t, c] - region[c, t, inside, :])

    wait_blocks(send_c, recv_c, send_c_sem, recv_c_sem, -1, True)
    unpack(recv_c, seam_writer(rotor_ghost, 0))
    seam_fix(rotor, rotor_new, mu_r, planes_r - 1, rotor_ghost)

    landed_shift.wait_recv()
    shifted(two_landed, cavity_ghost, width - offset)
    seam_fix(cavity, cavity_new, mu_c, 0, cavity_ghost)

    @pl.when(layer < layers - 1)
    def _():
        for piece in range(PIECES):
            edge_copy(0, piece, 1).wait_recv()
        edge_fix(high_own, high_got, rows - 1)

    @pl.when(layer > 0)
    def _():
        for piece in range(PIECES):
            edge_copy(1, piece, -1).wait_recv()
        edge_fix(low_own, low_got, 0)

    cavity_shift.wait_send()
    landed_shift.wait_send()
    wait_blocks(send_r, recv_r, send_r_sem, recv_r_sem, 1, False)
    wait_blocks(send_c, recv_c, send_c_sem, recv_c_sem, -1, False)
    for copy in col_copies:
        copy.wait_send()

    @pl.when(layer < layers - 1)
    def _():
        for piece in range(PIECES):
            edge_copy(1, piece, 1).wait_send()

    @pl.when(layer > 0)
    def _():
        for piece in range(PIECES):
            edge_copy(0, piece, -1).wait_send()


def relay(rotor_in, cavity_in, rotor_out, cavity_out, sem):
    copies = []
    for source, target in ((rotor_in, rotor_out), (cavity_in, cavity_out)):
        for t in range(source.shape[1]):
            copies.append(pltpu.make_async_copy(
                source.at[:, t], target.at[:, :, pl.ds(t * LANES, LANES)], sem.at[len(copies)]))
    for copy in copies:
        copy.start()
    for copy in copies:
        copy.wait()


def shards(sectors, rotor_state, cavity_state, block_map, rotor_offset):
    comps, planes_r, rows, width = rotor_state.shape
    planes_c = cavity_state.shape[1]
    tiles = width // LANES
    rotor = rotor_state.reshape(comps, planes_r * rows, width)
    cavity = cavity_state.reshape(comps, planes_c * rows, width)
    f32 = jnp.float32
    edge_rows = comps * tiles * (planes_r + planes_c)
    dma = pltpu.SemaphoreType.DMA
    hbm = pl.BlockSpec(memory_space=pltpu.HBM)
    anywhere = pl.BlockSpec(memory_space=pl.ANY)
    block = pltpu.VMEM((sectors, 16, LANES), f32)
    resident = pl.BlockSpec(memory_space=pltpu.VMEM)
    shape_r, shape_c = (comps, tiles, planes_r * rows, LANES), (comps, tiles, planes_c * rows, LANES)
    held_r, held_c = planes_r * rows + 2 * PAD, planes_c * rows + 2 * PAD
    edge = pltpu.VMEM((edge_rows, LANES), f32)
    columns = pltpu.VMEM((2, SUB, LANES), f32)
    rotor_new, cavity_new = pl.pallas_call(
        kernel,
        out_shape=(jax.ShapeDtypeStruct(shape_r, f32), jax.ShapeDtypeStruct(shape_c, f32)),
        in_specs=[hbm, pl.BlockSpec(memory_space=pltpu.SMEM), hbm, hbm],
        out_specs=(resident, resident),
        scratch_shapes=[
            pltpu.VMEM((comps, tiles, held_r, LANES), f32), pltpu.VMEM((comps, tiles, held_c, LANES), f32),
            pltpu.VMEM((tiles, held_r, LANES), f32), pltpu.VMEM((tiles, held_c, LANES), f32),
            pltpu.VMEM((tiles, held_r, LANES), f32), pltpu.VMEM((tiles, held_c, LANES), f32),
            pltpu.VMEM((2 * tiles, comps, rows, LANES), f32), pltpu.VMEM((2 * tiles, comps, rows, LANES), f32),
            pltpu.VMEM((tiles, comps, rows, LANES), f32), pltpu.VMEM((tiles, comps, rows, LANES), f32),
            block, block, block, block, block,
            edge, edge, edge, edge, columns, columns,
            pltpu.VMEM((SUB, LANES), jnp.int32), pltpu.SMEM((SUB, LANES), jnp.int32),
            pltpu.SMEM((sectors,), jnp.int32),
            dma((4 * tiles + 2,)), dma((sectors,)), dma((sectors,)), dma((sectors,)), dma((sectors,)),
            dma((2,)), dma((2,)), dma((2, PIECES)), dma((2, PIECES)), dma((2,)), dma((2,)),
        ],
        compiler_params=pltpu.CompilerParams(
            collective_id=0, has_side_effects=True, vmem_limit_bytes=24 * 1024 * 1024),
    )(pltpu.with_memory_space_constraint(block_map, pltpu.HBM), rotor_offset,
      *(pltpu.with_memory_space_constraint(x, pltpu.HBM) for x in (rotor, cavity)))
    rotor_next, cavity_next = pl.pallas_call(
        relay,
        out_shape=(jax.ShapeDtypeStruct(rotor.shape, f32), jax.ShapeDtypeStruct(cavity.shape, f32)),
        in_specs=[anywhere, anywhere],
        out_specs=(hbm, hbm),
        scratch_shapes=[dma((2 * tiles,))],
        compiler_params=pltpu.CompilerParams(vmem_limit_bytes=1024 * 1024),
    )(rotor_new, cavity_new)
    return rotor_next.reshape(rotor_state.shape), cavity_next.reshape(cavity_state.shape)


def solution(mesh):
    placed = (P(None, None, "layer", "sector"), P(None, None, "layer", "sector"), P(), P())
    return jax.shard_map(
        functools.partial(shards, mesh.shape["sector"]),
        mesh=mesh,
        in_specs=placed,
        out_specs=(P(None, None, "layer", "sector"), P(None, None, "layer", "sector")),
        check_vma=False,
    )
```

```python
import functools

import jax
import jax.numpy as jnp
from jax import lax
from jax.experimental import pallas as pl
from jax.experimental.pallas import tpu as pltpu
from jax.sharding import PartitionSpec as P

DIFFUSION = 0.05
LANES = 128
SUB = 8
PAD = 8
EDGE_ORDER = (0, 4, 1, 2, 3)
FIRST = 1
SECOND = 1
MESH = pl.DeviceIdType.MESH


def viscosity(density, energy):
    return 0.5 * jnp.exp(0.7 * jnp.log(energy / density))


def iota(axis):
    return lax.broadcasted_iota(jnp.int32, (SUB, LANES), axis)


def granule_transpose(x):
    sub, granule = iota(0), iota(1) // 16
    for bit in range(3):
        s, g = 1 << bit, 16 << bit
        a = (sub // s) % 2
        b = (granule // s) % 2
        up = pltpu.roll(pltpu.roll(x, g, axis=1), SUB - s, axis=0)
        down = pltpu.roll(pltpu.roll(x, LANES - g, axis=1), s, axis=0)
        x = jnp.where(a == b, x, jnp.where(b == 1, up, down))
    return x


def kernel(
    map_hbm, offset_ref, rotor_hbm, cavity_hbm, rotor_new, cavity_new,
    rotor, cavity, mu_r, mu_c, w_r, w_c,
    two_cavity, two_landed, rotor_ghost, cavity_ghost,
    packed, send_r, recv_r, send_c, recv_c,
    low_own, high_own, low_got, high_got, col_own, col_got, inverse_v, inverse,
    map_ref, load_sem, send_r_sem, recv_r_sem, send_c_sem, recv_c_sem, shift_send, shift_recv, edge_send, edge_recv,
    col_send, col_recv,
):
    sectors = lax.axis_size("sector")
    layers = lax.axis_size("layer")
    me = lax.axis_index("sector")
    layer = lax.axis_index("layer")
    comps, tiles, rows_r, _ = rotor_new.shape
    rows_c = cavity_new.shape[2]
    rows = two_cavity.shape[2]
    width = tiles * LANES
    planes_r, planes_c = rows_r // rows, rows_c // rows
    last_r = rows_r - rows
    used = comps * 2
    slot_rows = send_r.shape[1]
    packed_rows = packed.reshape(sectors * slot_rows, LANES)

    def sector_at(step):
        return {"sector": lax.rem(me + step + sectors, sectors)}

    barrier = pltpu.get_barrier_semaphore()

    @pl.when(layer > 0)
    def _():
        pl.semaphore_signal(barrier, inc=1, device_id={"layer": layer - 1}, device_id_type=MESH)

    @pl.when(layer < layers - 1)
    def _():
        pl.semaphore_signal(barrier, inc=1, device_id={"layer": layer + 1}, device_id_type=MESH)


    def greet(k, carry):
        pl.semaphore_signal(barrier, inc=1, device_id=sector_at(k), device_id_type=MESH)
        return carry

    lax.fori_loop(1, sectors, greet, 0)

    loads = []
    for t in range(tiles):
        loads.append(pltpu.make_async_copy(
            rotor_hbm.at[:, pl.ds(last_r, rows), pl.ds(t * LANES, LANES)], two_landed.at[t], load_sem.at[t]))
    for t in range(tiles):
        loads.append(pltpu.make_async_copy(
            cavity_hbm.at[:, pl.ds(0, rows), pl.ds(t * LANES, LANES)], two_cavity.at[t], load_sem.at[tiles + t]))
    for hbm, region, base in ((rotor_hbm, rotor, 2 * tiles), (cavity_hbm, cavity, 3 * tiles)):
        for t in range(tiles):
            loads.append(pltpu.make_async_copy(
                hbm.at[:, :, pl.ds(t * LANES, LANES)], region.at[:, t, pl.ds(PAD, hbm.shape[1])], load_sem.at[base + t]))
    map_load = pltpu.make_async_copy(map_hbm, map_ref, load_sem.at[4 * tiles + 1])
    map_load.start()
    for copy in loads:
        copy.start()

    def pack(read, send, recv):
        def one(t, carry):
            for q in range(used):
                packed_rows[pl.ds(SUB * slot_rows * t + q, SUB, stride=slot_rows), :] = granule_transpose(read(t, q))
            return carry

        lax.fori_loop(0, tiles, one, 0)

        recv[0] = packed[inverse[0, 0]]

        def slot(k, carry):
            send[k] = packed[inverse[0, k]]
            return carry

        lax.fori_loop(1, sectors, slot, 0)

    def unpack(recv, write):
        def block(j, carry):
            packed[j] = recv[map_ref[j]]
            return carry

        lax.fori_loop(0, sectors, block, 0)

        def one(t, carry):
            for q in range(used):
                write(t, q, granule_transpose(packed_rows[pl.ds(SUB * slot_rows * t + q, SUB, stride=slot_rows), :]))
            return carry

        lax.fori_loop(0, tiles, one, 0)

    def seam_reader(buffer):
        return lambda t, q: buffer[t, q // 2, pl.ds(SUB * (q % 2), SUB), :]

    def seam_writer(buffer, base):
        def write(t, q, value):
            buffer[base + t, q // 2, pl.ds(SUB * (q % 2), SUB), :] = value

        return write

    def block_copy(send, recv, send_sem, recv_sem, k, sign):
        return pltpu.make_async_remote_copy(
            src_ref=send.at[k, pl.ds(0, used)], dst_ref=recv.at[k, pl.ds(0, used)],
            send_sem=send_sem.at[k], recv_sem=recv_sem.at[k],
            device_id=sector_at(sign * k), device_id_type=MESH)

    def start_blocks(send, recv, send_sem, recv_sem, sign):
        def one(k, carry):
            block_copy(send, recv, send_sem, recv_sem, k, sign).start()
            return carry

        lax.fori_loop(1, sectors, one, 0)

    def wait_blocks(send, recv, send_sem, recv_sem, sign, arrived):
        def one(k, carry):
            copy = block_copy(send, recv, send_sem, recv_sem, k, sign)
            if arrived:
                copy.wait_recv()
            else:
                copy.wait_send()
            return carry

        lax.fori_loop(1, sectors, one, 0)

    def shift_copy(buffer, source, target, index, step):
        return pltpu.make_async_remote_copy(
            src_ref=buffer.at[pl.ds(source, tiles)], dst_ref=buffer.at[pl.ds(target, tiles)],
            send_sem=shift_send.at[index], recv_sem=shift_recv.at[index],
            device_id=sector_at(step), device_id_type=MESH)

    def shifted(buffer, target, start):
        tile0 = lax.div(start, jnp.int32(LANES))
        rest = lax.rem(start, jnp.int32(LANES))
        back = lax.rem(LANES - rest, jnp.int32(LANES))
        keep = lax.broadcasted_iota(jnp.int32, (rows, LANES), 1) < LANES - rest
        for t in range(tiles):
            i0 = tile0 + t
            i1 = jnp.minimum(i0 + 1, 2 * tiles - 1)
            for c in range(comps):
                here = pltpu.roll(buffer[i0, c], back, axis=1)
                after = pltpu.roll(buffer[i1, c], back, axis=1)
                target[t, c] = jnp.where(keep, here, after)

    offset = offset_ref[0]

    def edge_copy(upward, c, step):
        source, target = (high_own, low_got) if upward else (low_own, high_got)
        at = pl.ds(c * piece, piece)
        return pltpu.make_async_remote_copy(
            src_ref=source.at[at], dst_ref=target.at[at],
            send_sem=edge_send.at[upward, c], recv_sem=edge_recv.at[upward, c],
            device_id={"layer": lax.rem(layer + step + layers, layers)}, device_id_type=MESH)

    def start_edges(low, high):
        @pl.when(layer < layers - 1)
        def _():
            for c in EDGE_ORDER[low:high]:
                edge_copy(1, c, 1).start()

        @pl.when(layer > 0)
        def _():
            for c in EDGE_ORDER[low:high]:
                edge_copy(0, c, -1).start()

    map_load.wait()

    found = jnp.zeros((SUB, LANES), jnp.int32)
    for j in range(sectors):
        found = jnp.where(iota(1) == map_ref[j], j, found)
    inverse_v[...] = found

    to_scalar = pltpu.make_async_copy(inverse_v, inverse, load_sem.at[4 * tiles])
    to_scalar.start()

    for t in range(tiles):
        loads[t].wait()
    to_scalar.wait()
    pack(seam_reader(two_landed), send_r, recv_r)
    for t in range(tiles):
        loads[tiles + t].wait()
    for region in (rotor, cavity):
        for c in range(comps):
            for t in range(tiles):
                region[c, t, pl.ds(0, PAD), :] = jnp.zeros((PAD, LANES), jnp.float32)
                region[c, t, pl.ds(region.shape[2] - PAD, PAD), :] = jnp.zeros((PAD, LANES), jnp.float32)

    pl.semaphore_wait(barrier, sectors - 1 + jnp.where(layer > 0, 1, 0) + jnp.where(layer < layers - 1, 1, 0))

    cavity_shift = shift_copy(two_cavity, 0, tiles, 0, -1)
    cavity_shift.start()
    start_blocks(send_r, recv_r, send_r_sem, recv_r_sem, 1)

    for copy in loads[2 * tiles:]:
        copy.wait()
    piece = tiles * (planes_r + planes_c)
    parts = ((rotor, rotor_new, planes_r, 0), (cavity, cavity_new, planes_c, tiles * planes_r))
    for edge, own in ((0, low_own), (rows - 1, high_own)):
        for c in range(comps):
            for region, _, planes, base in parts:
                for t in range(tiles):
                    own[pl.ds(c * piece + base + t * planes, planes), :] = region[
                        c, t, pl.ds(PAD + edge, planes, stride=rows), :]

    start_edges(0, FIRST)

    lane = iota(1)
    pieces = []
    for c in range(comps):
        for region, new, planes in ((rotor, rotor_new, planes_r), (cavity, cavity_new, planes_c)):
            for p in range(planes):
                for half in range(2):
                    pieces.append((region, new, c, p * rows + half * SUB))
    group = len(pieces) // comps
    zero = jnp.zeros((SUB, LANES), jnp.float32)
    head, tail = zero, zero
    for v, (region, _, c, r) in enumerate(pieces):
        head = jnp.where(lane == v, region[c, 0, pl.ds(PAD + r, SUB), :][:, 0:1], head)
        tail = jnp.where(lane == v, region[c, tiles - 1, pl.ds(PAD + r, SUB), :][:, LANES - 1:], tail)
    col_own[0] = head
    col_own[1] = tail
    col_copies = [
        pltpu.make_async_remote_copy(
            src_ref=col_own.at[i], dst_ref=col_got.at[i], send_sem=col_send.at[i], recv_sem=col_recv.at[i],
            device_id=sector_at(-1 if i == 0 else 1), device_id_type=MESH)
        for i in range(2)
    ]
    for copy in col_copies:
        copy.start()

    rate = jnp.float32(DIFFUSION)
    half_rate = jnp.float32(0.5 * DIFFUSION)
    row = lax.broadcasted_iota(jnp.int32, (rows, LANES), 0)
    column = lax.broadcasted_iota(jnp.int32, (rows, LANES), 1)

    def interior(region, new, mu, w, planes):
        def first(p, carry):
            at = pl.ds(pl.multiple_of(PAD + p * rows, SUB), rows)
            for t in range(tiles):
                density = region[0, t, at, :]
                mu[t, at, :] = viscosity(density, region[4, t, at, :])
                w[t, at, :] = region[3, t, at, :] / density
            return carry

        lax.fori_loop(0, planes, first, 0)

        def one(p, carry):
            base = pl.multiple_of(PAD + p * rows, SUB)
            at = pl.ds(base, rows)
            upper, lower = pl.ds(base + 1, rows), pl.ds(base - 1, rows)
            above = pl.ds(pl.multiple_of(PAD + jnp.minimum(p + 1, planes - 1) * rows, SUB), rows)
            below = pl.ds(pl.multiple_of(PAD + jnp.maximum(p - 1, 0) * rows, SUB), rows)
            rate_above = jnp.where(p < planes - 1, half_rate, 0.0)
            rate_below = jnp.where(p > 0, half_rate, 0.0)

            def after(ref, t):
                x = ref[t, at, :]
                if t < tiles - 1:
                    x = jnp.where(column == 0, ref[t + 1, at, :], x)
                return pltpu.roll(x, LANES - 1, axis=1)

            def before(ref, t):
                x = ref[t, at, :]
                if t > 0:
                    x = jnp.where(column == LANES - 1, ref[t - 1, at, :], x)
                return pltpu.roll(x, 1, axis=1)

            for t in range(tiles):
                m = mu[t, at, :]
                up = rate_above * (m + mu[t, above, :])
                down = rate_below * (m + mu[t, below, :])
                out = jnp.where(row == rows - 1, 0.0, half_rate * (m + mu[t, upper, :]))
                inn = jnp.where(row == 0, 0.0, half_rate * (m + mu[t, lower, :]))
                east = half_rate * (m + after(mu, t))
                west = half_rate * (m + before(mu, t))
                wind_east = rate * after(w, t)
                wind_west = rate * before(w, t)
                if t == tiles - 1:
                    east = jnp.where(column == LANES - 1, 0.0, east)
                    wind_east = jnp.where(column == LANES - 1, 0.0, wind_east)
                if t == 0:
                    west = jnp.where(column == 0, 0.0, west)
                    wind_west = jnp.where(column == 0, 0.0, wind_west)
                centre = 1.0 - ((up + down) + (out + inn) + (east + west))
                east = east - wind_east
                west = west + wind_west
                for c in range(comps):
                    values = region.at[c]
                    total = centre * values[t, at, :]
                    total = total + (up * values[t, above, :] + down * values[t, below, :])
                    total = total + (out * values[t, upper, :] + inn * values[t, lower, :])
                    total = total + (east * after(values, t) + west * before(values, t))
                    new[c, t, pl.ds(pl.multiple_of(p * rows, rows), rows), :] = total
            return carry

        lax.fori_loop(0, planes, one, 0)

    interior(rotor, rotor_new, mu_r, w_r, planes_r)
    interior(cavity, cavity_new, mu_c, w_c, planes_c)

    cavity_shift.wait_recv()
    shifted(two_cavity, rotor_ghost, offset)
    pack(seam_reader(rotor_ghost), send_c, recv_c)
    start_blocks(send_c, recv_c, send_c_sem, recv_c_sem, -1)

    start_edges(FIRST, SECOND)

    wait_blocks(send_r, recv_r, send_r_sem, recv_r_sem, 1, True)
    unpack(recv_r, seam_writer(two_landed, tiles))
    landed_shift = shift_copy(two_landed, tiles, 0, 1, 1)
    landed_shift.start()
    start_edges(SECOND, comps)

    def edge_factor(own, got, base, size):
        a, b = ([ref[pl.ds(c * piece + base, size), :] for c in (0, 4)] for ref in (own, got))
        return half_rate * (viscosity(*a) + viscosity(*b))

    def edge_fix(own, got, edge, c, factors):
        for (_, new, planes, base), factor in zip(parts, factors):
            at = pl.ds(c * piece + base, tiles * planes)
            change = factor * (got[at, :] - own[at, :])
            for t in range(tiles):
                at = (c, t, pl.ds(edge, planes, stride=rows), slice(None))
                new[at] = new[at] + change[t * planes:(t + 1) * planes]

    def edges(own, got, edge, upward, step):
        for c in EDGE_ORDER[:2]:
            edge_copy(upward, c, step).wait_recv()
        factors = [edge_factor(own, got, base, tiles * planes) for _, _, planes, base in parts]
        for n, c in enumerate(EDGE_ORDER):
            if n > 1:
                edge_copy(upward, c, step).wait_recv()
            edge_fix(own, got, edge, c, factors)

    for copy in col_copies:
        copy.wait_recv()

    def spread(x, shift):
        one = jnp.where(lane < group, pltpu.roll(x, LANES - shift, axis=1) if shift else x, 0.0)
        out = one
        for c in range(1, comps):
            out = out + pltpu.roll(one, c * group, axis=1)
        return out

    def column_state(x):
        density, momentum, energy = spread(x, 0), spread(x, 3 * group), spread(x, 4 * group)
        live = lane < comps * group
        density = jnp.where(live, density, 1.0)
        energy = jnp.where(live, energy, 1.0)
        return viscosity(density, energy), momentum / density

    states = {}
    for name, x in (("head", col_own[0]), ("tail", col_own[1]), ("after", col_got[0]), ("before", col_got[1])):
        states[name] = (x, *column_state(x))

    def column_face(a, b):
        (qa, ma, wa), (qb, mb, wb) = states[a], states[b]
        return half_rate * (ma + mb) * (qb - qa), rate * wb * qb

    def column_change(own, other, sign):
        diffused, carried = column_face(own, other)
        return diffused - sign * carried

    at_tail = column_change("tail", "after", 1.0)
    at_head = column_change("head", "before", -1.0)
    for v, (_, new, c, r) in enumerate(pieces):
        at = (c, tiles - 1, pl.ds(r, SUB), slice(None))
        new[at] = new[at] + jnp.where(lane == LANES - 1, at_tail[:, v:v + 1], 0.0)
        at = (c, 0, pl.ds(r, SUB), slice(None))
        new[at] = new[at] + jnp.where(lane == 0, at_head[:, v:v + 1], 0.0)

    def seam_fix(region, new, mu, p, ghost):
        for t in range(tiles):
            inside = pl.ds(PAD + p * rows, rows)
            factor = half_rate * (viscosity(ghost[t, 0], ghost[t, 4]) + mu[t, inside, :])
            for c in range(comps):
                at = (c, t, pl.ds(p * rows, rows), slice(None))
                new[at] = new[at] + factor * (ghost[t, c] - region[c, t, inside, :])

    wait_blocks(send_c, recv_c, send_c_sem, recv_c_sem, -1, True)
    unpack(recv_c, seam_writer(rotor_ghost, 0))
    seam_fix(rotor, rotor_new, mu_r, planes_r - 1, rotor_ghost)

    cavity_shift.wait_send()
    wait_blocks(send_r, recv_r, send_r_sem, recv_r_sem, 1, False)
    wait_blocks(send_c, recv_c, send_c_sem, recv_c_sem, -1, False)
    for copy in col_copies:
        copy.wait_send()

    landed_shift.wait_recv()
    shifted(two_landed, cavity_ghost, width - offset)
    seam_fix(cavity, cavity_new, mu_c, 0, cavity_ghost)
    landed_shift.wait_send()

    @pl.when(layer < layers - 1)
    def _():
        for c in range(comps):
            edge_copy(1, c, 1).wait_send()

    @pl.when(layer > 0)
    def _():
        for c in range(comps):
            edge_copy(0, c, -1).wait_send()

    @pl.when(layer < layers - 1)
    def _():
        edges(high_own, high_got, rows - 1, 0, 1)

    @pl.when(layer > 0)
    def _():
        edges(low_own, low_got, 0, 1, -1)


def relay(rotor_in, cavity_in, rotor_out, cavity_out, sem):
    copies = []
    for source, target in ((rotor_in, rotor_out), (cavity_in, cavity_out)):
        for t in range(source.shape[1]):
            copies.append(pltpu.make_async_copy(
                source.at[:, t], target.at[:, :, pl.ds(t * LANES, LANES)], sem.at[len(copies)]))
    for copy in copies:
        copy.start()
    for copy in copies:
        copy.wait()


def shards(sectors, rotor_state, cavity_state, block_map, rotor_offset):
    comps, planes_r, rows, width = rotor_state.shape
    planes_c = cavity_state.shape[1]
    tiles = width // LANES
    rotor = rotor_state.reshape(comps, planes_r * rows, width)
    cavity = cavity_state.reshape(comps, planes_c * rows, width)
    f32 = jnp.float32
    edge_rows = comps * tiles * (planes_r + planes_c)
    dma = pltpu.SemaphoreType.DMA
    hbm = pl.BlockSpec(memory_space=pltpu.HBM)
    anywhere = pl.BlockSpec(memory_space=pl.ANY)
    block = pltpu.VMEM((sectors, 16, LANES), f32)
    resident = pl.BlockSpec(memory_space=pltpu.VMEM)
    shape_r, shape_c = (comps, tiles, planes_r * rows, LANES), (comps, tiles, planes_c * rows, LANES)
    held_r, held_c = planes_r * rows + 2 * PAD, planes_c * rows + 2 * PAD
    edge = pltpu.VMEM((edge_rows, LANES), f32)
    columns = pltpu.VMEM((2, SUB, LANES), f32)
    rotor_new, cavity_new = pl.pallas_call(
        kernel,
        out_shape=(jax.ShapeDtypeStruct(shape_r, f32), jax.ShapeDtypeStruct(shape_c, f32)),
        in_specs=[hbm, pl.BlockSpec(memory_space=pltpu.SMEM), hbm, hbm],
        out_specs=(resident, resident),
        scratch_shapes=[
            pltpu.VMEM((comps, tiles, held_r, LANES), f32), pltpu.VMEM((comps, tiles, held_c, LANES), f32),
            pltpu.VMEM((tiles, held_r, LANES), f32), pltpu.VMEM((tiles, held_c, LANES), f32),
            pltpu.VMEM((tiles, held_r, LANES), f32), pltpu.VMEM((tiles, held_c, LANES), f32),
            pltpu.VMEM((2 * tiles, comps, rows, LANES), f32), pltpu.VMEM((2 * tiles, comps, rows, LANES), f32),
            pltpu.VMEM((tiles, comps, rows, LANES), f32), pltpu.VMEM((tiles, comps, rows, LANES), f32),
            block, block, block, block, block,
            edge, edge, edge, edge, columns, columns,
            pltpu.VMEM((SUB, LANES), jnp.int32), pltpu.SMEM((SUB, LANES), jnp.int32),
            pltpu.SMEM((sectors,), jnp.int32),
            dma((4 * tiles + 2,)), dma((sectors,)), dma((sectors,)), dma((sectors,)), dma((sectors,)),
            dma((2,)), dma((2,)), dma((2, comps)), dma((2, comps)), dma((2,)), dma((2,)),
        ],
        compiler_params=pltpu.CompilerParams(
            collective_id=0, has_side_effects=True, vmem_limit_bytes=24 * 1024 * 1024),
    )(pltpu.with_memory_space_constraint(block_map, pltpu.HBM), rotor_offset,
      *(pltpu.with_memory_space_constraint(x, pltpu.HBM) for x in (rotor, cavity)))
    rotor_next, cavity_next = pl.pallas_call(
        relay,
        out_shape=(jax.ShapeDtypeStruct(rotor.shape, f32), jax.ShapeDtypeStruct(cavity.shape, f32)),
        in_specs=[anywhere, anywhere],
        out_specs=(hbm, hbm),
        scratch_shapes=[dma((2 * tiles,))],
        compiler_params=pltpu.CompilerParams(vmem_limit_bytes=1024 * 1024),
    )(rotor_new, cavity_new)
    return rotor_next.reshape(rotor_state.shape), cavity_next.reshape(cavity_state.shape)


def solution(mesh):
    placed = (P(None, None, "layer", "sector"), P(None, None, "layer", "sector"), P(), P())
    return jax.shard_map(
        functools.partial(shards, mesh.shape["sector"]),
        mesh=mesh,
        in_specs=placed,
        out_specs=(P(None, None, "layer", "sector"), P(None, None, "layer", "sector")),
        check_vma=False,
    )
```

```python
import functools

import jax
import jax.numpy as jnp
from jax import lax
from jax.experimental import pallas as pl
from jax.experimental.pallas import tpu as pltpu
from jax.sharding import PartitionSpec as P

DIFFUSION = 0.05
LANES = 128
SUB = 8
PAD = 8
EDGE_ORDER = (0, 4, 1, 2, 3)
FIRST = 1
SECOND = 1
RELAYED = (3,)
MESH = pl.DeviceIdType.MESH


def viscosity(density, energy):
    return 0.5 * jnp.exp(0.7 * jnp.log(energy / density))


def iota(axis):
    return lax.broadcasted_iota(jnp.int32, (SUB, LANES), axis)


def granule_transpose(x):
    sub, granule = iota(0), iota(1) // 16
    for bit in range(3):
        s, g = 1 << bit, 16 << bit
        a = (sub // s) % 2
        b = (granule // s) % 2
        up = pltpu.roll(pltpu.roll(x, g, axis=1), SUB - s, axis=0)
        down = pltpu.roll(pltpu.roll(x, LANES - g, axis=1), s, axis=0)
        x = jnp.where(a == b, x, jnp.where(b == 1, up, down))
    return x


def kernel(
    map_hbm, offset_ref, rotor_hbm, cavity_hbm, rotor_new, cavity_new,
    rotor, cavity, mu_r, mu_c, w_r, w_c,
    two_cavity, two_landed, rotor_ghost, cavity_ghost,
    packed, send_r, recv_r, send_c, recv_c,
    low_own, high_own, low_got, high_got, col_own, col_got, inverse_v, inverse,
    map_ref, load_sem, send_r_sem, recv_r_sem, send_c_sem, recv_c_sem, shift_send, shift_recv, edge_send, edge_recv,
    col_send, col_recv, way_got, way_send, way_recv,
):
    sectors = lax.axis_size("sector")
    layers = lax.axis_size("layer")
    me = lax.axis_index("sector")
    layer = lax.axis_index("layer")
    comps, tiles, rows_r, _ = rotor_new.shape
    rows_c = cavity_new.shape[2]
    rows = two_cavity.shape[2]
    width = tiles * LANES
    planes_r, planes_c = rows_r // rows, rows_c // rows
    last_r = rows_r - rows
    used = comps * 2
    slot_rows = send_r.shape[1]
    packed_rows = packed.reshape(sectors * slot_rows, LANES)

    def sector_at(step):
        return {"sector": lax.rem(me + step + sectors, sectors)}

    barrier = pltpu.get_barrier_semaphore()

    @pl.when(layer > 0)
    def _():
        pl.semaphore_signal(barrier, inc=1, device_id={"layer": layer - 1}, device_id_type=MESH)

    @pl.when(layer < layers - 1)
    def _():
        pl.semaphore_signal(barrier, inc=1, device_id={"layer": layer + 1}, device_id_type=MESH)


    @pl.when(layer == 0)
    def _():
        pl.semaphore_signal(barrier, inc=1, device_id={"layer": layer + 2}, device_id_type=MESH)

    @pl.when(layer == layers - 1)
    def _():
        pl.semaphore_signal(barrier, inc=1, device_id={"layer": layer - 2}, device_id_type=MESH)

    def greet(k, carry):
        pl.semaphore_signal(barrier, inc=1, device_id=sector_at(k), device_id_type=MESH)
        return carry

    lax.fori_loop(1, sectors, greet, 0)

    loads = []
    for t in range(tiles):
        loads.append(pltpu.make_async_copy(
            rotor_hbm.at[:, pl.ds(last_r, rows), pl.ds(t * LANES, LANES)], two_landed.at[t], load_sem.at[t]))
    for t in range(tiles):
        loads.append(pltpu.make_async_copy(
            cavity_hbm.at[:, pl.ds(0, rows), pl.ds(t * LANES, LANES)], two_cavity.at[t], load_sem.at[tiles + t]))
    for hbm, region, base in ((rotor_hbm, rotor, 2 * tiles), (cavity_hbm, cavity, 3 * tiles)):
        for t in range(tiles):
            loads.append(pltpu.make_async_copy(
                hbm.at[:, :, pl.ds(t * LANES, LANES)], region.at[:, t, pl.ds(PAD, hbm.shape[1])], load_sem.at[base + t]))
    map_load = pltpu.make_async_copy(map_hbm, map_ref, load_sem.at[4 * tiles + 1])
    map_load.start()
    for copy in loads:
        copy.start()

    def pack(read, send, recv):
        def one(t, carry):
            for q in range(used):
                packed_rows[pl.ds(SUB * slot_rows * t + q, SUB, stride=slot_rows), :] = granule_transpose(read(t, q))
            return carry

        lax.fori_loop(0, tiles, one, 0)

        recv[0] = packed[inverse[0, 0]]

        def slot(k, carry):
            send[k] = packed[inverse[0, k]]
            return carry

        lax.fori_loop(1, sectors, slot, 0)

    def unpack(recv, write):
        def block(j, carry):
            packed[j] = recv[map_ref[j]]
            return carry

        lax.fori_loop(0, sectors, block, 0)

        def one(t, carry):
            for q in range(used):
                write(t, q, granule_transpose(packed_rows[pl.ds(SUB * slot_rows * t + q, SUB, stride=slot_rows), :]))
            return carry

        lax.fori_loop(0, tiles, one, 0)

    def seam_reader(buffer):
        return lambda t, q: buffer[t, q // 2, pl.ds(SUB * (q % 2), SUB), :]

    def seam_writer(buffer, base):
        def write(t, q, value):
            buffer[base + t, q // 2, pl.ds(SUB * (q % 2), SUB), :] = value

        return write

    def block_copy(send, recv, send_sem, recv_sem, k, sign):
        return pltpu.make_async_remote_copy(
            src_ref=send.at[k, pl.ds(0, used)], dst_ref=recv.at[k, pl.ds(0, used)],
            send_sem=send_sem.at[k], recv_sem=recv_sem.at[k],
            device_id=sector_at(sign * k), device_id_type=MESH)

    def start_blocks(send, recv, send_sem, recv_sem, sign):
        def one(k, carry):
            block_copy(send, recv, send_sem, recv_sem, k, sign).start()
            return carry

        lax.fori_loop(1, sectors, one, 0)

    def wait_blocks(send, recv, send_sem, recv_sem, sign, arrived):
        def one(k, carry):
            copy = block_copy(send, recv, send_sem, recv_sem, k, sign)
            if arrived:
                copy.wait_recv()
            else:
                copy.wait_send()
            return carry

        lax.fori_loop(1, sectors, one, 0)

    def shift_copy(buffer, source, target, index, step):
        return pltpu.make_async_remote_copy(
            src_ref=buffer.at[pl.ds(source, tiles)], dst_ref=buffer.at[pl.ds(target, tiles)],
            send_sem=shift_send.at[index], recv_sem=shift_recv.at[index],
            device_id=sector_at(step), device_id_type=MESH)

    def shifted(buffer, target, start):
        tile0 = lax.div(start, jnp.int32(LANES))
        rest = lax.rem(start, jnp.int32(LANES))
        back = lax.rem(LANES - rest, jnp.int32(LANES))
        keep = lax.broadcasted_iota(jnp.int32, (rows, LANES), 1) < LANES - rest
        for t in range(tiles):
            i0 = tile0 + t
            i1 = jnp.minimum(i0 + 1, 2 * tiles - 1)
            for c in range(comps):
                here = pltpu.roll(buffer[i0, c], back, axis=1)
                after = pltpu.roll(buffer[i1, c], back, axis=1)
                target[t, c] = jnp.where(keep, here, after)

    offset = offset_ref[0]

    def edge_copy(upward, c, step):
        source, target = (high_own, low_got) if upward else (low_own, high_got)
        at = pl.ds(c * piece, piece)
        return pltpu.make_async_remote_copy(
            src_ref=source.at[at], dst_ref=target.at[at],
            send_sem=edge_send.at[upward, c], recv_sem=edge_recv.at[upward, c],
            device_id={"layer": lax.rem(layer + step + layers, layers)}, device_id_type=MESH)

    by_way_up, by_way_down = layer == layers - 3, layer == 2
    way_up, way_down = layer == layers - 1, layer == 0
    has_up = layer < layers - 1
    has_down = layer > 0

    def way_copy(upward, n):
        source = high_own if upward else low_own
        return pltpu.make_async_remote_copy(
            src_ref=source.at[pl.ds(RELAYED[n] * piece, piece)], dst_ref=way_got.at[pl.ds(n * piece, piece)],
            send_sem=way_send.at[n], recv_sem=way_recv.at[n],
            device_id={"layer": lax.rem(layer + (2 if upward else -2) + layers, layers)}, device_id_type=MESH)

    def way_pass(upward, n):
        target = low_got if upward else high_got
        return pltpu.make_async_remote_copy(
            src_ref=way_got.at[pl.ds(n * piece, piece)], dst_ref=target.at[pl.ds(RELAYED[n] * piece, piece)],
            send_sem=way_send.at[n], recv_sem=edge_recv.at[upward, RELAYED[n]],
            device_id={"layer": lax.rem(layer + (-1 if upward else 1) + layers, layers)}, device_id_type=MESH)

    def each_way(upward, at, act):
        @pl.when(at)
        def _():
            for n in range(len(RELAYED)):
                act(upward, n)

    def each_edge(group, act):
        direct = [c for c in group if c not in RELAYED]
        others = [c for c in group if c in RELAYED]
        for upward, has, by_way, step in ((1, has_up, by_way_up, 1), (0, has_down, by_way_down, -1)):
            @pl.when(has)
            def _():
                for c in direct:
                    act(edge_copy(upward, c, step))

            if others:
                @pl.when(jnp.logical_and(has, jnp.logical_not(by_way)))
                def _():
                    for c in others:
                        act(edge_copy(upward, c, step))

    def start_edges(low, high):
        each_edge(EDGE_ORDER[low:high], lambda copy: copy.start())

    def start_way(upward, n):
        way_copy(upward, n).start()

    def pass_way(upward, n):
        way_copy(upward, n).wait_recv()
        way_pass(upward, n).start()

    map_load.wait()

    found = jnp.zeros((SUB, LANES), jnp.int32)
    for j in range(sectors):
        found = jnp.where(iota(1) == map_ref[j], j, found)
    inverse_v[...] = found

    to_scalar = pltpu.make_async_copy(inverse_v, inverse, load_sem.at[4 * tiles])
    to_scalar.start()

    for t in range(tiles):
        loads[t].wait()
    to_scalar.wait()
    pack(seam_reader(two_landed), send_r, recv_r)
    for t in range(tiles):
        loads[tiles + t].wait()
    for region in (rotor, cavity):
        for c in range(comps):
            for t in range(tiles):
                region[c, t, pl.ds(0, PAD), :] = jnp.zeros((PAD, LANES), jnp.float32)
                region[c, t, pl.ds(region.shape[2] - PAD, PAD), :] = jnp.zeros((PAD, LANES), jnp.float32)

    pl.semaphore_wait(barrier, sectors - 1 + jnp.where(layer > 0, 1, 0) + jnp.where(layer < layers - 1, 1, 0)
                      + jnp.where(jnp.logical_or(layer == 2, layer == layers - 3), 1, 0))

    cavity_shift = shift_copy(two_cavity, 0, tiles, 0, -1)
    start_blocks(send_r, recv_r, send_r_sem, recv_r_sem, 1)
    cavity_shift.start()

    for copy in loads[2 * tiles:]:
        copy.wait()
    piece = tiles * (planes_r + planes_c)
    parts = ((rotor, rotor_new, planes_r, 0), (cavity, cavity_new, planes_c, tiles * planes_r))
    for edge, own in ((0, low_own), (rows - 1, high_own)):
        for c in range(comps):
            for region, _, planes, base in parts:
                for t in range(tiles):
                    own[pl.ds(c * piece + base + t * planes, planes), :] = region[
                        c, t, pl.ds(PAD + edge, planes, stride=rows), :]

    start_edges(0, FIRST)
    each_way(1, by_way_up, start_way)
    each_way(0, by_way_down, start_way)

    lane = iota(1)
    pieces = []
    for c in range(comps):
        for region, new, planes in ((rotor, rotor_new, planes_r), (cavity, cavity_new, planes_c)):
            for p in range(planes):
                for half in range(2):
                    pieces.append((region, new, c, p * rows + half * SUB))
    group = len(pieces) // comps
    zero = jnp.zeros((SUB, LANES), jnp.float32)
    head, tail = zero, zero
    for v, (region, _, c, r) in enumerate(pieces):
        head = jnp.where(lane == v, region[c, 0, pl.ds(PAD + r, SUB), :][:, 0:1], head)
        tail = jnp.where(lane == v, region[c, tiles - 1, pl.ds(PAD + r, SUB), :][:, LANES - 1:], tail)
    col_own[0] = head
    col_own[1] = tail
    col_copies = [
        pltpu.make_async_remote_copy(
            src_ref=col_own.at[i], dst_ref=col_got.at[i], send_sem=col_send.at[i], recv_sem=col_recv.at[i],
            device_id=sector_at(-1 if i == 0 else 1), device_id_type=MESH)
        for i in range(2)
    ]
    for copy in col_copies:
        copy.start()

    rate = jnp.float32(DIFFUSION)
    half_rate = jnp.float32(0.5 * DIFFUSION)
    row = lax.broadcasted_iota(jnp.int32, (rows, LANES), 0)
    column = lax.broadcasted_iota(jnp.int32, (rows, LANES), 1)

    def interior(region, new, mu, w, planes):
        def first(p, carry):
            at = pl.ds(pl.multiple_of(PAD + p * rows, SUB), rows)
            for t in range(tiles):
                density = region[0, t, at, :]
                mu[t, at, :] = viscosity(density, region[4, t, at, :])
                w[t, at, :] = region[3, t, at, :] / density
            return carry

        lax.fori_loop(0, planes, first, 0)

        def one(p, carry):
            base = pl.multiple_of(PAD + p * rows, SUB)
            at = pl.ds(base, rows)
            upper, lower = pl.ds(base + 1, rows), pl.ds(base - 1, rows)
            above = pl.ds(pl.multiple_of(PAD + jnp.minimum(p + 1, planes - 1) * rows, SUB), rows)
            below = pl.ds(pl.multiple_of(PAD + jnp.maximum(p - 1, 0) * rows, SUB), rows)
            rate_above = jnp.where(p < planes - 1, half_rate, 0.0)
            rate_below = jnp.where(p > 0, half_rate, 0.0)

            def after(ref, t):
                x = ref[t, at, :]
                if t < tiles - 1:
                    x = jnp.where(column == 0, ref[t + 1, at, :], x)
                return pltpu.roll(x, LANES - 1, axis=1)

            def before(ref, t):
                x = ref[t, at, :]
                if t > 0:
                    x = jnp.where(column == LANES - 1, ref[t - 1, at, :], x)
                return pltpu.roll(x, 1, axis=1)

            for t in range(tiles):
                m = mu[t, at, :]
                up = rate_above * (m + mu[t, above, :])
                down = rate_below * (m + mu[t, below, :])
                out = jnp.where(row == rows - 1, 0.0, half_rate * (m + mu[t, upper, :]))
                inn = jnp.where(row == 0, 0.0, half_rate * (m + mu[t, lower, :]))
                east = half_rate * (m + after(mu, t))
                west = half_rate * (m + before(mu, t))
                wind_east = rate * after(w, t)
                wind_west = rate * before(w, t)
                if t == tiles - 1:
                    east = jnp.where(column == LANES - 1, 0.0, east)
                    wind_east = jnp.where(column == LANES - 1, 0.0, wind_east)
                if t == 0:
                    west = jnp.where(column == 0, 0.0, west)
                    wind_west = jnp.where(column == 0, 0.0, wind_west)
                centre = 1.0 - ((up + down) + (out + inn) + (east + west))
                east = east - wind_east
                west = west + wind_west
                for c in range(comps):
                    values = region.at[c]
                    total = centre * values[t, at, :]
                    total = total + (up * values[t, above, :] + down * values[t, below, :])
                    total = total + (out * values[t, upper, :] + inn * values[t, lower, :])
                    total = total + (east * after(values, t) + west * before(values, t))
                    new[c, t, pl.ds(pl.multiple_of(p * rows, rows), rows), :] = total
            return carry

        lax.fori_loop(0, planes, one, 0)

    interior(rotor, rotor_new, mu_r, w_r, planes_r)
    interior(cavity, cavity_new, mu_c, w_c, planes_c)

    cavity_shift.wait_recv()
    shifted(two_cavity, rotor_ghost, offset)
    pack(seam_reader(rotor_ghost), send_c, recv_c)
    start_blocks(send_c, recv_c, send_c_sem, recv_c_sem, -1)

    start_edges(FIRST, SECOND)

    wait_blocks(send_r, recv_r, send_r_sem, recv_r_sem, 1, True)
    unpack(recv_r, seam_writer(two_landed, tiles))
    landed_shift = shift_copy(two_landed, tiles, 0, 1, 1)
    landed_shift.start()
    start_edges(SECOND, comps)
    each_way(1, way_up, pass_way)
    each_way(0, way_down, pass_way)

    def edge_factor(own, got, base, size):
        a, b = ([ref[pl.ds(c * piece + base, size), :] for c in (0, 4)] for ref in (own, got))
        return half_rate * (viscosity(*a) + viscosity(*b))

    def edge_fix(own, got, edge, c, factors):
        for (_, new, planes, base), factor in zip(parts, factors):
            at = pl.ds(c * piece + base, tiles * planes)
            change = factor * (got[at, :] - own[at, :])
            for t in range(tiles):
                at = (c, t, pl.ds(edge, planes, stride=rows), slice(None))
                new[at] = new[at] + change[t * planes:(t + 1) * planes]

    def edges(own, got, edge, upward, step):
        for c in EDGE_ORDER[:2]:
            edge_copy(upward, c, step).wait_recv()
        factors = [edge_factor(own, got, base, tiles * planes) for _, _, planes, base in parts]
        for n, c in enumerate(EDGE_ORDER):
            if n > 1:
                edge_copy(upward, c, step).wait_recv()
            edge_fix(own, got, edge, c, factors)

    for copy in col_copies:
        copy.wait_recv()

    def spread(x, shift):
        one = jnp.where(lane < group, pltpu.roll(x, LANES - shift, axis=1) if shift else x, 0.0)
        out = one
        for c in range(1, comps):
            out = out + pltpu.roll(one, c * group, axis=1)
        return out

    def column_state(x):
        density, momentum, energy = spread(x, 0), spread(x, 3 * group), spread(x, 4 * group)
        live = lane < comps * group
        density = jnp.where(live, density, 1.0)
        energy = jnp.where(live, energy, 1.0)
        return viscosity(density, energy), momentum / density

    states = {}
    for name, x in (("head", col_own[0]), ("tail", col_own[1]), ("after", col_got[0]), ("before", col_got[1])):
        states[name] = (x, *column_state(x))

    def column_face(a, b):
        (qa, ma, wa), (qb, mb, wb) = states[a], states[b]
        return half_rate * (ma + mb) * (qb - qa), rate * wb * qb

    def column_change(own, other, sign):
        diffused, carried = column_face(own, other)
        return diffused - sign * carried

    at_tail = column_change("tail", "after", 1.0)
    at_head = column_change("head", "before", -1.0)
    for v, (_, new, c, r) in enumerate(pieces):
        at = (c, tiles - 1, pl.ds(r, SUB), slice(None))
        new[at] = new[at] + jnp.where(lane == LANES - 1, at_tail[:, v:v + 1], 0.0)
        at = (c, 0, pl.ds(r, SUB), slice(None))
        new[at] = new[at] + jnp.where(lane == 0, at_head[:, v:v + 1], 0.0)

    def seam_fix(region, new, mu, p, ghost):
        for t in range(tiles):
            inside = pl.ds(PAD + p * rows, rows)
            factor = half_rate * (viscosity(ghost[t, 0], ghost[t, 4]) + mu[t, inside, :])
            for c in range(comps):
                at = (c, t, pl.ds(p * rows, rows), slice(None))
                new[at] = new[at] + factor * (ghost[t, c] - region[c, t, inside, :])

    wait_blocks(send_c, recv_c, send_c_sem, recv_c_sem, -1, True)
    unpack(recv_c, seam_writer(rotor_ghost, 0))
    seam_fix(rotor, rotor_new, mu_r, planes_r - 1, rotor_ghost)

    cavity_shift.wait_send()
    wait_blocks(send_r, recv_r, send_r_sem, recv_r_sem, 1, False)
    wait_blocks(send_c, recv_c, send_c_sem, recv_c_sem, -1, False)
    for copy in col_copies:
        copy.wait_send()

    landed_shift.wait_recv()
    shifted(two_landed, cavity_ghost, width - offset)
    seam_fix(cavity, cavity_new, mu_c, 0, cavity_ghost)
    landed_shift.wait_send()

    each_edge(EDGE_ORDER, lambda copy: copy.wait_send())
    each_way(1, by_way_up, lambda upward, n: way_copy(upward, n).wait_send())
    each_way(0, by_way_down, lambda upward, n: way_copy(upward, n).wait_send())
    each_way(1, way_up, lambda upward, n: way_pass(upward, n).wait_send())
    each_way(0, way_down, lambda upward, n: way_pass(upward, n).wait_send())

    @pl.when(layer < layers - 1)
    def _():
        edges(high_own, high_got, rows - 1, 0, 1)

    @pl.when(layer > 0)
    def _():
        edges(low_own, low_got, 0, 1, -1)


def relay(rotor_in, cavity_in, rotor_out, cavity_out, sem):
    copies = []
    for source, target in ((rotor_in, rotor_out), (cavity_in, cavity_out)):
        for t in range(source.shape[1]):
            copies.append(pltpu.make_async_copy(
                source.at[:, t], target.at[:, :, pl.ds(t * LANES, LANES)], sem.at[len(copies)]))
    for copy in copies:
        copy.start()
    for copy in copies:
        copy.wait()


def shards(sectors, rotor_state, cavity_state, block_map, rotor_offset):
    comps, planes_r, rows, width = rotor_state.shape
    planes_c = cavity_state.shape[1]
    tiles = width // LANES
    rotor = rotor_state.reshape(comps, planes_r * rows, width)
    cavity = cavity_state.reshape(comps, planes_c * rows, width)
    f32 = jnp.float32
    edge_rows = comps * tiles * (planes_r + planes_c)
    dma = pltpu.SemaphoreType.DMA
    hbm = pl.BlockSpec(memory_space=pltpu.HBM)
    anywhere = pl.BlockSpec(memory_space=pl.ANY)
    block = pltpu.VMEM((sectors, 16, LANES), f32)
    resident = pl.BlockSpec(memory_space=pltpu.VMEM)
    shape_r, shape_c = (comps, tiles, planes_r * rows, LANES), (comps, tiles, planes_c * rows, LANES)
    held_r, held_c = planes_r * rows + 2 * PAD, planes_c * rows + 2 * PAD
    edge = pltpu.VMEM((edge_rows, LANES), f32)
    columns = pltpu.VMEM((2, SUB, LANES), f32)
    rotor_new, cavity_new = pl.pallas_call(
        kernel,
        out_shape=(jax.ShapeDtypeStruct(shape_r, f32), jax.ShapeDtypeStruct(shape_c, f32)),
        in_specs=[hbm, pl.BlockSpec(memory_space=pltpu.SMEM), hbm, hbm],
        out_specs=(resident, resident),
        scratch_shapes=[
            pltpu.VMEM((comps, tiles, held_r, LANES), f32), pltpu.VMEM((comps, tiles, held_c, LANES), f32),
            pltpu.VMEM((tiles, held_r, LANES), f32), pltpu.VMEM((tiles, held_c, LANES), f32),
            pltpu.VMEM((tiles, held_r, LANES), f32), pltpu.VMEM((tiles, held_c, LANES), f32),
            pltpu.VMEM((2 * tiles, comps, rows, LANES), f32), pltpu.VMEM((2 * tiles, comps, rows, LANES), f32),
            pltpu.VMEM((tiles, comps, rows, LANES), f32), pltpu.VMEM((tiles, comps, rows, LANES), f32),
            block, block, block, block, block,
            edge, edge, edge, edge, columns, columns,
            pltpu.VMEM((SUB, LANES), jnp.int32), pltpu.SMEM((SUB, LANES), jnp.int32),
            pltpu.SMEM((sectors,), jnp.int32),
            dma((4 * tiles + 2,)), dma((sectors,)), dma((sectors,)), dma((sectors,)), dma((sectors,)),
            dma((2,)), dma((2,)), dma((2, comps)), dma((2, comps)), dma((2,)), dma((2,)),
            pltpu.VMEM((edge_rows // comps * len(RELAYED), LANES), f32), dma((len(RELAYED),)), dma((len(RELAYED),)),
        ],
        compiler_params=pltpu.CompilerParams(
            collective_id=0, has_side_effects=True, vmem_limit_bytes=24 * 1024 * 1024),
    )(pltpu.with_memory_space_constraint(block_map, pltpu.HBM), rotor_offset,
      *(pltpu.with_memory_space_constraint(x, pltpu.HBM) for x in (rotor, cavity)))
    rotor_next, cavity_next = pl.pallas_call(
        relay,
        out_shape=(jax.ShapeDtypeStruct(rotor.shape, f32), jax.ShapeDtypeStruct(cavity.shape, f32)),
        in_specs=[anywhere, anywhere],
        out_specs=(hbm, hbm),
        scratch_shapes=[dma((2 * tiles,))],
        compiler_params=pltpu.CompilerParams(vmem_limit_bytes=1024 * 1024),
    )(rotor_new, cavity_new)
    return rotor_next.reshape(rotor_state.shape), cavity_next.reshape(cavity_state.shape)


def solution(mesh):
    placed = (P(None, None, "layer", "sector"), P(None, None, "layer", "sector"), P(), P())
    return jax.shard_map(
        functools.partial(shards, mesh.shape["sector"]),
        mesh=mesh,
        in_specs=placed,
        out_specs=(P(None, None, "layer", "sector"), P(None, None, "layer", "sector")),
        check_vma=False,
    )
```

```python
import functools

import jax
import jax.numpy as jnp
from jax import lax
from jax.experimental import pallas as pl
from jax.experimental.pallas import tpu as pltpu
from jax.sharding import PartitionSpec as P

DIFFUSION = 0.05
LANES = 128
SUB = 8
PAD = 8
EDGE_ORDER = (0, 4, 1, 2, 3)
FIRST = 1
SECOND = 2
RELAYED = (3,)
MESH = pl.DeviceIdType.MESH


def viscosity(density, energy):
    return 0.5 * jnp.exp(0.7 * jnp.log(energy / density))


def iota(axis):
    return lax.broadcasted_iota(jnp.int32, (SUB, LANES), axis)


def granule_transpose(x):
    sub, granule = iota(0), iota(1) // 16
    for bit in range(3):
        s, g = 1 << bit, 16 << bit
        a = (sub // s) % 2
        b = (granule // s) % 2
        up = pltpu.roll(pltpu.roll(x, g, axis=1), SUB - s, axis=0)
        down = pltpu.roll(pltpu.roll(x, LANES - g, axis=1), s, axis=0)
        x = jnp.where(a == b, x, jnp.where(b == 1, up, down))
    return x


def kernel(
    map_hbm, offset_ref, rotor_hbm, cavity_hbm, rotor_new, cavity_new,
    rotor, cavity, mu_r, mu_c, w_r, w_c,
    two_cavity, two_landed, rotor_ghost, cavity_ghost,
    packed, send_r, recv_r, send_c, recv_c,
    low_own, high_own, low_got, high_got, col_own, col_got, inverse_v, inverse,
    map_ref, load_sem, send_r_sem, recv_r_sem, send_c_sem, recv_c_sem, shift_send, shift_recv, edge_send, edge_recv,
    col_send, col_recv, way_got, way_send, way_recv,
):
    sectors = lax.axis_size("sector")
    layers = lax.axis_size("layer")
    me = lax.axis_index("sector")
    layer = lax.axis_index("layer")
    comps, tiles, rows_r, _ = rotor_new.shape
    rows_c = cavity_new.shape[2]
    rows = two_cavity.shape[2]
    width = tiles * LANES
    planes_r, planes_c = rows_r // rows, rows_c // rows
    last_r = rows_r - rows
    used = comps * 2
    slot_rows = send_r.shape[1]
    packed_rows = packed.reshape(sectors * slot_rows, LANES)

    def sector_at(step):
        return {"sector": lax.rem(me + step + sectors, sectors)}

    barrier = pltpu.get_barrier_semaphore()

    @pl.when(layer > 0)
    def _():
        pl.semaphore_signal(barrier, inc=1, device_id={"layer": layer - 1}, device_id_type=MESH)

    @pl.when(layer < layers - 1)
    def _():
        pl.semaphore_signal(barrier, inc=1, device_id={"layer": layer + 1}, device_id_type=MESH)


    @pl.when(layer == 0)
    def _():
        pl.semaphore_signal(barrier, inc=1, device_id={"layer": layer + 2}, device_id_type=MESH)

    @pl.when(layer == layers - 1)
    def _():
        pl.semaphore_signal(barrier, inc=1, device_id={"layer": layer - 2}, device_id_type=MESH)

    def greet(k, carry):
        pl.semaphore_signal(barrier, inc=1, device_id=sector_at(k), device_id_type=MESH)
        return carry

    lax.fori_loop(1, sectors, greet, 0)

    loads = []
    for t in range(tiles):
        loads.append(pltpu.make_async_copy(
            rotor_hbm.at[:, pl.ds(last_r, rows), pl.ds(t * LANES, LANES)], two_landed.at[t], load_sem.at[t]))
    for t in range(tiles):
        loads.append(pltpu.make_async_copy(
            cavity_hbm.at[:, pl.ds(0, rows), pl.ds(t * LANES, LANES)], two_cavity.at[t], load_sem.at[tiles + t]))
    for hbm, region, base in ((rotor_hbm, rotor, 2 * tiles), (cavity_hbm, cavity, 3 * tiles)):
        for t in range(tiles):
            loads.append(pltpu.make_async_copy(
                hbm.at[:, :, pl.ds(t * LANES, LANES)], region.at[:, t, pl.ds(PAD, hbm.shape[1])], load_sem.at[base + t]))
    map_load = pltpu.make_async_copy(map_hbm, map_ref, load_sem.at[4 * tiles + 1])
    map_load.start()
    for copy in loads:
        copy.start()

    def pack(read, send, recv):
        def one(t, carry):
            for q in range(used):
                packed_rows[pl.ds(SUB * slot_rows * t + q, SUB, stride=slot_rows), :] = granule_transpose(read(t, q))
            return carry

        lax.fori_loop(0, tiles, one, 0)

        recv[0] = packed[inverse[0, 0]]

        def slot(k, carry):
            send[k] = packed[inverse[0, k]]
            return carry

        lax.fori_loop(1, sectors, slot, 0)

    def unpack(recv, write):
        def block(j, carry):
            packed[j] = recv[map_ref[j]]
            return carry

        lax.fori_loop(0, sectors, block, 0)

        def one(t, carry):
            for q in range(used):
                write(t, q, granule_transpose(packed_rows[pl.ds(SUB * slot_rows * t + q, SUB, stride=slot_rows), :]))
            return carry

        lax.fori_loop(0, tiles, one, 0)

    def seam_reader(buffer):
        return lambda t, q: buffer[t, q // 2, pl.ds(SUB * (q % 2), SUB), :]

    def seam_writer(buffer, base):
        def write(t, q, value):
            buffer[base + t, q // 2, pl.ds(SUB * (q % 2), SUB), :] = value

        return write

    def block_copy(send, recv, send_sem, recv_sem, k, sign):
        return pltpu.make_async_remote_copy(
            src_ref=send.at[k, pl.ds(0, used)], dst_ref=recv.at[k, pl.ds(0, used)],
            send_sem=send_sem.at[k], recv_sem=recv_sem.at[k],
            device_id=sector_at(sign * k), device_id_type=MESH)

    def start_blocks(send, recv, send_sem, recv_sem, sign):
        def one(k, carry):
            block_copy(send, recv, send_sem, recv_sem, k, sign).start()
            return carry

        lax.fori_loop(1, sectors, one, 0)

    def wait_blocks(send, recv, send_sem, recv_sem, sign, arrived):
        def one(k, carry):
            copy = block_copy(send, recv, send_sem, recv_sem, k, sign)
            if arrived:
                copy.wait_recv()
            else:
                copy.wait_send()
            return carry

        lax.fori_loop(1, sectors, one, 0)

    def shift_copy(buffer, source, target, index, step):
        return pltpu.make_async_remote_copy(
            src_ref=buffer.at[pl.ds(source, tiles)], dst_ref=buffer.at[pl.ds(target, tiles)],
            send_sem=shift_send.at[index], recv_sem=shift_recv.at[index],
            device_id=sector_at(step), device_id_type=MESH)

    def shifted(buffer, target, start):
        tile0 = lax.div(start, jnp.int32(LANES))
        rest = lax.rem(start, jnp.int32(LANES))
        back = lax.rem(LANES - rest, jnp.int32(LANES))
        keep = lax.broadcasted_iota(jnp.int32, (rows, LANES), 1) < LANES - rest
        for t in range(tiles):
            i0 = tile0 + t
            i1 = jnp.minimum(i0 + 1, 2 * tiles - 1)
            for c in range(comps):
                here = pltpu.roll(buffer[i0, c], back, axis=1)
                after = pltpu.roll(buffer[i1, c], back, axis=1)
                target[t, c] = jnp.where(keep, here, after)

    offset = offset_ref[0]

    def edge_copy(upward, c, step):
        source, target = (high_own, low_got) if upward else (low_own, high_got)
        at = pl.ds(c * piece, piece)
        return pltpu.make_async_remote_copy(
            src_ref=source.at[at], dst_ref=target.at[at],
            send_sem=edge_send.at[upward, c], recv_sem=edge_recv.at[upward, c],
            device_id={"layer": lax.rem(layer + step + layers, layers)}, device_id_type=MESH)

    by_way_up, by_way_down = layer == layers - 3, layer == 2
    way_up, way_down = layer == layers - 1, layer == 0
    has_up = layer < layers - 1
    has_down = layer > 0

    def way_copy(upward, n):
        source = high_own if upward else low_own
        return pltpu.make_async_remote_copy(
            src_ref=source.at[pl.ds(RELAYED[n] * piece, piece)], dst_ref=way_got.at[pl.ds(n * piece, piece)],
            send_sem=way_send.at[n], recv_sem=way_recv.at[n],
            device_id={"layer": lax.rem(layer + (2 if upward else -2) + layers, layers)}, device_id_type=MESH)

    def way_pass(upward, n):
        target = low_got if upward else high_got
        return pltpu.make_async_remote_copy(
            src_ref=way_got.at[pl.ds(n * piece, piece)], dst_ref=target.at[pl.ds(RELAYED[n] * piece, piece)],
            send_sem=way_send.at[n], recv_sem=edge_recv.at[upward, RELAYED[n]],
            device_id={"layer": lax.rem(layer + (-1 if upward else 1) + layers, layers)}, device_id_type=MESH)

    def each_way(upward, at, act):
        @pl.when(at)
        def _():
            for n in range(len(RELAYED)):
                act(upward, n)

    def each_edge(group, act):
        direct = [c for c in group if c not in RELAYED]
        others = [c for c in group if c in RELAYED]
        for upward, has, by_way, step in ((1, has_up, by_way_up, 1), (0, has_down, by_way_down, -1)):
            @pl.when(has)
            def _():
                for c in direct:
                    act(edge_copy(upward, c, step))

            if others:
                @pl.when(jnp.logical_and(has, jnp.logical_not(by_way)))
                def _():
                    for c in others:
                        act(edge_copy(upward, c, step))

    def start_edges(low, high):
        each_edge(EDGE_ORDER[low:high], lambda copy: copy.start())

    def start_way(upward, n):
        way_copy(upward, n).start()

    def pass_way(upward, n):
        way_copy(upward, n).wait_recv()
        way_pass(upward, n).start()

    map_load.wait()

    found = jnp.zeros((SUB, LANES), jnp.int32)
    for j in range(sectors):
        found = jnp.where(iota(1) == map_ref[j], j, found)
    inverse_v[...] = found

    to_scalar = pltpu.make_async_copy(inverse_v, inverse, load_sem.at[4 * tiles])
    to_scalar.start()

    for t in range(tiles):
        loads[t].wait()
    to_scalar.wait()
    pack(seam_reader(two_landed), send_r, recv_r)
    for t in range(tiles):
        loads[tiles + t].wait()
    for region in (rotor, cavity):
        for c in range(comps):
            for t in range(tiles):
                region[c, t, pl.ds(0, PAD), :] = jnp.zeros((PAD, LANES), jnp.float32)
                region[c, t, pl.ds(region.shape[2] - PAD, PAD), :] = jnp.zeros((PAD, LANES), jnp.float32)

    pl.semaphore_wait(barrier, sectors - 1 + jnp.where(layer > 0, 1, 0) + jnp.where(layer < layers - 1, 1, 0)
                      + jnp.where(jnp.logical_or(layer == 2, layer == layers - 3), 1, 0))

    cavity_shift = shift_copy(two_cavity, 0, tiles, 0, -1)
    start_blocks(send_r, recv_r, send_r_sem, recv_r_sem, 1)
    cavity_shift.start()

    for copy in loads[2 * tiles:]:
        copy.wait()
    piece = tiles * (planes_r + planes_c)
    parts = ((rotor, rotor_new, planes_r, 0), (cavity, cavity_new, planes_c, tiles * planes_r))
    for edge, own in ((0, low_own), (rows - 1, high_own)):
        for c in range(comps):
            for region, _, planes, base in parts:
                for t in range(tiles):
                    own[pl.ds(c * piece + base + t * planes, planes), :] = region[
                        c, t, pl.ds(PAD + edge, planes, stride=rows), :]

    start_edges(0, FIRST)
    each_way(1, by_way_up, start_way)
    each_way(0, by_way_down, start_way)

    lane = iota(1)
    pieces = []
    for c in range(comps):
        for region, new, planes in ((rotor, rotor_new, planes_r), (cavity, cavity_new, planes_c)):
            for p in range(planes):
                for half in range(2):
                    pieces.append((region, new, c, p * rows + half * SUB))
    group = len(pieces) // comps
    zero = jnp.zeros((SUB, LANES), jnp.float32)
    head, tail = zero, zero
    for v, (region, _, c, r) in enumerate(pieces):
        head = jnp.where(lane == v, region[c, 0, pl.ds(PAD + r, SUB), :][:, 0:1], head)
        tail = jnp.where(lane == v, region[c, tiles - 1, pl.ds(PAD + r, SUB), :][:, LANES - 1:], tail)
    col_own[0] = head
    col_own[1] = tail
    col_copies = [
        pltpu.make_async_remote_copy(
            src_ref=col_own.at[i], dst_ref=col_got.at[i], send_sem=col_send.at[i], recv_sem=col_recv.at[i],
            device_id=sector_at(-1 if i == 0 else 1), device_id_type=MESH)
        for i in range(2)
    ]
    for copy in col_copies:
        copy.start()

    rate = jnp.float32(DIFFUSION)
    half_rate = jnp.float32(0.5 * DIFFUSION)
    row = lax.broadcasted_iota(jnp.int32, (rows, LANES), 0)
    column = lax.broadcasted_iota(jnp.int32, (rows, LANES), 1)

    def interior(region, new, mu, w, planes):
        def first(p, carry):
            at = pl.ds(pl.multiple_of(PAD + p * rows, SUB), rows)
            for t in range(tiles):
                density = region[0, t, at, :]
                mu[t, at, :] = viscosity(density, region[4, t, at, :])
                w[t, at, :] = region[3, t, at, :] / density
            return carry

        lax.fori_loop(0, planes, first, 0)

        def one(p, carry):
            base = pl.multiple_of(PAD + p * rows, SUB)
            at = pl.ds(base, rows)
            upper, lower = pl.ds(base + 1, rows), pl.ds(base - 1, rows)
            above = pl.ds(pl.multiple_of(PAD + jnp.minimum(p + 1, planes - 1) * rows, SUB), rows)
            below = pl.ds(pl.multiple_of(PAD + jnp.maximum(p - 1, 0) * rows, SUB), rows)
            rate_above = jnp.where(p < planes - 1, half_rate, 0.0)
            rate_below = jnp.where(p > 0, half_rate, 0.0)

            def after(ref, t):
                x = ref[t, at, :]
                if t < tiles - 1:
                    x = jnp.where(column == 0, ref[t + 1, at, :], x)
                return pltpu.roll(x, LANES - 1, axis=1)

            def before(ref, t):
                x = ref[t, at, :]
                if t > 0:
                    x = jnp.where(column == LANES - 1, ref[t - 1, at, :], x)
                return pltpu.roll(x, 1, axis=1)

            for t in range(tiles):
                m = mu[t, at, :]
                up = rate_above * (m + mu[t, above, :])
                down = rate_below * (m + mu[t, below, :])
                out = jnp.where(row == rows - 1, 0.0, half_rate * (m + mu[t, upper, :]))
                inn = jnp.where(row == 0, 0.0, half_rate * (m + mu[t, lower, :]))
                east = half_rate * (m + after(mu, t))
                west = half_rate * (m + before(mu, t))
                wind_east = rate * after(w, t)
                wind_west = rate * before(w, t)
                if t == tiles - 1:
                    east = jnp.where(column == LANES - 1, 0.0, east)
                    wind_east = jnp.where(column == LANES - 1, 0.0, wind_east)
                if t == 0:
                    west = jnp.where(column == 0, 0.0, west)
                    wind_west = jnp.where(column == 0, 0.0, wind_west)
                centre = 1.0 - ((up + down) + (out + inn) + (east + west))
                east = east - wind_east
                west = west + wind_west
                for c in range(comps):
                    values = region.at[c]
                    total = centre * values[t, at, :]
                    total = total + (up * values[t, above, :] + down * values[t, below, :])
                    total = total + (out * values[t, upper, :] + inn * values[t, lower, :])
                    total = total + (east * after(values, t) + west * before(values, t))
                    new[c, t, pl.ds(pl.multiple_of(p * rows, rows), rows), :] = total
            return carry

        lax.fori_loop(0, planes, one, 0)

    interior(rotor, rotor_new, mu_r, w_r, planes_r)
    interior(cavity, cavity_new, mu_c, w_c, planes_c)

    cavity_shift.wait_recv()
    shifted(two_cavity, rotor_ghost, offset)
    pack(seam_reader(rotor_ghost), send_c, recv_c)
    start_blocks(send_c, recv_c, send_c_sem, recv_c_sem, -1)

    start_edges(FIRST, SECOND)

    wait_blocks(send_r, recv_r, send_r_sem, recv_r_sem, 1, True)
    unpack(recv_r, seam_writer(two_landed, tiles))
    landed_shift = shift_copy(two_landed, tiles, 0, 1, 1)
    landed_shift.start()
    start_edges(SECOND, comps)
    each_way(1, way_up, pass_way)
    each_way(0, way_down, pass_way)

    def edge_factor(own, got, base, size):
        a, b = ([ref[pl.ds(c * piece + base, size), :] for c in (0, 4)] for ref in (own, got))
        return half_rate * (viscosity(*a) + viscosity(*b))

    def edge_fix(own, got, edge, c, factors):
        for (_, new, planes, base), factor in zip(parts, factors):
            at = pl.ds(c * piece + base, tiles * planes)
            change = factor * (got[at, :] - own[at, :])
            for t in range(tiles):
                at = (c, t, pl.ds(edge, planes, stride=rows), slice(None))
                new[at] = new[at] + change[t * planes:(t + 1) * planes]

    def edges(own, got, edge, upward, step):
        for c in EDGE_ORDER[:2]:
            edge_copy(upward, c, step).wait_recv()
        factors = [edge_factor(own, got, base, tiles * planes) for _, _, planes, base in parts]
        for n, c in enumerate(EDGE_ORDER):
            if n > 1:
                edge_copy(upward, c, step).wait_recv()
            edge_fix(own, got, edge, c, factors)

    for copy in col_copies:
        copy.wait_recv()

    def spread(x, shift):
        one = jnp.where(lane < group, pltpu.roll(x, LANES - shift, axis=1) if shift else x, 0.0)
        out = one
        for c in range(1, comps):
            out = out + pltpu.roll(one, c * group, axis=1)
        return out

    def column_state(x):
        density, momentum, energy = spread(x, 0), spread(x, 3 * group), spread(x, 4 * group)
        live = lane < comps * group
        density = jnp.where(live, density, 1.0)
        energy = jnp.where(live, energy, 1.0)
        return viscosity(density, energy), momentum / density

    states = {}
    for name, x in (("head", col_own[0]), ("tail", col_own[1]), ("after", col_got[0]), ("before", col_got[1])):
        states[name] = (x, *column_state(x))

    def column_face(a, b):
        (qa, ma, wa), (qb, mb, wb) = states[a], states[b]
        return half_rate * (ma + mb) * (qb - qa), rate * wb * qb

    def column_change(own, other, sign):
        diffused, carried = column_face(own, other)
        return diffused - sign * carried

    at_tail = column_change("tail", "after", 1.0)
    at_head = column_change("head", "before", -1.0)
    for v, (_, new, c, r) in enumerate(pieces):
        at = (c, tiles - 1, pl.ds(r, SUB), slice(None))
        new[at] = new[at] + jnp.where(lane == LANES - 1, at_tail[:, v:v + 1], 0.0)
        at = (c, 0, pl.ds(r, SUB), slice(None))
        new[at] = new[at] + jnp.where(lane == 0, at_head[:, v:v + 1], 0.0)

    def seam_fix(region, new, mu, p, ghost):
        for t in range(tiles):
            inside = pl.ds(PAD + p * rows, rows)
            factor = half_rate * (viscosity(ghost[t, 0], ghost[t, 4]) + mu[t, inside, :])
            for c in range(comps):
                at = (c, t, pl.ds(p * rows, rows), slice(None))
                new[at] = new[at] + factor * (ghost[t, c] - region[c, t, inside, :])

    wait_blocks(send_c, recv_c, send_c_sem, recv_c_sem, -1, True)
    unpack(recv_c, seam_writer(rotor_ghost, 0))
    seam_fix(rotor, rotor_new, mu_r, planes_r - 1, rotor_ghost)

    cavity_shift.wait_send()
    wait_blocks(send_r, recv_r, send_r_sem, recv_r_sem, 1, False)
    wait_blocks(send_c, recv_c, send_c_sem, recv_c_sem, -1, False)
    for copy in col_copies:
        copy.wait_send()

    landed_shift.wait_recv()
    shifted(two_landed, cavity_ghost, width - offset)
    seam_fix(cavity, cavity_new, mu_c, 0, cavity_ghost)
    landed_shift.wait_send()

    each_edge(EDGE_ORDER, lambda copy: copy.wait_send())
    each_way(1, by_way_up, lambda upward, n: way_copy(upward, n).wait_send())
    each_way(0, by_way_down, lambda upward, n: way_copy(upward, n).wait_send())
    each_way(1, way_up, lambda upward, n: way_pass(upward, n).wait_send())
    each_way(0, way_down, lambda upward, n: way_pass(upward, n).wait_send())

    @pl.when(layer < layers - 1)
    def _():
        edges(high_own, high_got, rows - 1, 0, 1)

    @pl.when(layer > 0)
    def _():
        edges(low_own, low_got, 0, 1, -1)


def relay(rotor_in, cavity_in, rotor_out, cavity_out, sem):
    copies = []
    for source, target in ((rotor_in, rotor_out), (cavity_in, cavity_out)):
        for t in range(source.shape[1]):
            copies.append(pltpu.make_async_copy(
                source.at[:, t], target.at[:, :, pl.ds(t * LANES, LANES)], sem.at[len(copies)]))
    for copy in copies:
        copy.start()
    for copy in copies:
        copy.wait()


def shards(sectors, rotor_state, cavity_state, block_map, rotor_offset):
    comps, planes_r, rows, width = rotor_state.shape
    planes_c = cavity_state.shape[1]
    tiles = width // LANES
    rotor = rotor_state.reshape(comps, planes_r * rows, width)
    cavity = cavity_state.reshape(comps, planes_c * rows, width)
    f32 = jnp.float32
    edge_rows = comps * tiles * (planes_r + planes_c)
    dma = pltpu.SemaphoreType.DMA
    hbm = pl.BlockSpec(memory_space=pltpu.HBM)
    anywhere = pl.BlockSpec(memory_space=pl.ANY)
    block = pltpu.VMEM((sectors, 16, LANES), f32)
    resident = pl.BlockSpec(memory_space=pltpu.VMEM)
    shape_r, shape_c = (comps, tiles, planes_r * rows, LANES), (comps, tiles, planes_c * rows, LANES)
    held_r, held_c = planes_r * rows + 2 * PAD, planes_c * rows + 2 * PAD
    edge = pltpu.VMEM((edge_rows, LANES), f32)
    columns = pltpu.VMEM((2, SUB, LANES), f32)
    rotor_new, cavity_new = pl.pallas_call(
        kernel,
        out_shape=(jax.ShapeDtypeStruct(shape_r, f32), jax.ShapeDtypeStruct(shape_c, f32)),
        in_specs=[hbm, pl.BlockSpec(memory_space=pltpu.SMEM), hbm, hbm],
        out_specs=(resident, resident),
        scratch_shapes=[
            pltpu.VMEM((comps, tiles, held_r, LANES), f32), pltpu.VMEM((comps, tiles, held_c, LANES), f32),
            pltpu.VMEM((tiles, held_r, LANES), f32), pltpu.VMEM((tiles, held_c, LANES), f32),
            pltpu.VMEM((tiles, held_r, LANES), f32), pltpu.VMEM((tiles, held_c, LANES), f32),
            pltpu.VMEM((2 * tiles, comps, rows, LANES), f32), pltpu.VMEM((2 * tiles, comps, rows, LANES), f32),
            pltpu.VMEM((tiles, comps, rows, LANES), f32), pltpu.VMEM((tiles, comps, rows, LANES), f32),
            block, block, block, block, block,
            edge, edge, edge, edge, columns, columns,
            pltpu.VMEM((SUB, LANES), jnp.int32), pltpu.SMEM((SUB, LANES), jnp.int32),
            pltpu.SMEM((sectors,), jnp.int32),
            dma((4 * tiles + 2,)), dma((sectors,)), dma((sectors,)), dma((sectors,)), dma((sectors,)),
            dma((2,)), dma((2,)), dma((2, comps)), dma((2, comps)), dma((2,)), dma((2,)),
            pltpu.VMEM((edge_rows // comps * len(RELAYED), LANES), f32), dma((len(RELAYED),)), dma((len(RELAYED),)),
        ],
        compiler_params=pltpu.CompilerParams(
            collective_id=0, has_side_effects=True, vmem_limit_bytes=24 * 1024 * 1024),
    )(pltpu.with_memory_space_constraint(block_map, pltpu.HBM), rotor_offset,
      *(pltpu.with_memory_space_constraint(x, pltpu.HBM) for x in (rotor, cavity)))
    rotor_next, cavity_next = pl.pallas_call(
        relay,
        out_shape=(jax.ShapeDtypeStruct(rotor.shape, f32), jax.ShapeDtypeStruct(cavity.shape, f32)),
        in_specs=[anywhere, anywhere],
        out_specs=(hbm, hbm),
        scratch_shapes=[dma((2 * tiles,))],
        compiler_params=pltpu.CompilerParams(vmem_limit_bytes=1024 * 1024),
    )(rotor_new, cavity_new)
    return rotor_next.reshape(rotor_state.shape), cavity_next.reshape(cavity_state.shape)


def solution(mesh):
    placed = (P(None, None, "layer", "sector"), P(None, None, "layer", "sector"), P(), P())
    return jax.shard_map(
        functools.partial(shards, mesh.shape["sector"]),
        mesh=mesh,
        in_specs=placed,
        out_specs=(P(None, None, "layer", "sector"), P(None, None, "layer", "sector")),
        check_vma=False,
    )
```
